512 devices in a mesh: lvl: 128 (over y, z_hi, x), col: 4 (over z_lo, core).
Axes of the slice: x: 4, y: 8, z: 8 (z_hi: 4, z_lo: 2; z = z_hi * 2 + z_lo), core: 2. Of those that a mesh axis runs over, the one named last changes fastest.
Arguments:
- up_blocks: float32 [256, 512, 512], P('lvl', None, 'col'), may hold values from -1.25 to 1.25
- level_blocks: float32 [256, 512, 512], P('lvl', None, 'col'), may hold values from -11 to 2, as said below
- down_blocks: float32 [256, 512, 512], P('lvl', None, 'col'), may hold values from -1.25 to 1.25
Outputs:
- reduced_level: float32 [128, 512, 512], P('lvl', None, 'col')
- reduced_up: float32 [128, 512, 512], P('lvl', None, 'col')
- reduced_down: float32 [128, 512, 512], P('lvl', None, 'col')
The draws below stay inside these ranges and needn't reach their ends.
Inputs may be any that keep to these rules, and one draw needn't show every extreme that they name: `level_blocks`: every diagonal entry of every level's block is -1 or less.
All inputs are finite; a program needn't handle non-finite values.
Results may differ from the reference program's by a relative error of at most 0.00013.
Values sent between devices are 32-bit elements; how exact they have to be, the bound alone decides.
A program may use at most 64 MiB of HBM per device.

```python
import math
import jax
import jax.numpy as jnp
from jax import lax

P_SIZE = 512
SWEEPS = 2
LEVELS = 256


def draw_level_blocks(key, part):
    key_entries, key_spread, key_peak, key_height = jax.random.split(jax.random.fold_in(key, 17), 4)
    random_part = jnp.clip(jax.random.normal(key_entries, (LEVELS, P_SIZE, P_SIZE), jnp.float32), -4.0, 4.0)
    peak_scale = jax.random.uniform(key_height, (), jnp.float32, 1.0, 1.5)
    spread = jax.random.uniform(key_spread, (LEVELS, P_SIZE), jnp.float32)
    peak_level = jax.random.randint(key_peak, (), 0, LEVELS)
    level_rank = lax.broadcasted_iota(jnp.float32, (LEVELS, 1, 1), 0)
    level_number = lax.broadcasted_iota(jnp.int32, (LEVELS, 1, 1), 0)
    factor = 1.0 + 2.0 * level_rank / max(LEVELS - 1, 1)
    factor = jnp.where(level_number == peak_level, 3.0 * peak_scale, factor)
    coupling = 0.8 * factor * random_part / math.sqrt(P_SIZE)
    diagonal_values = -factor[:, :, 0] * (1.0 + 0.5 * spread)
    row_index = lax.broadcasted_iota(jnp.int32, (P_SIZE, P_SIZE), 0)
    col_index = lax.broadcasted_iota(jnp.int32, (P_SIZE, P_SIZE), 1)
    return jnp.where(row_index == col_index, diagonal_values[:, :, None], coupling)


def shard_levels(stream_key, shape, shards, smallest, high):
    factor_of = 1.0
    for axis_at, shards_of in shards:
        steps = jax.random.uniform(jax.random.fold_in(jax.random.fold_in(stream_key, 6), axis_at), (shards_of,), jnp.float32, smallest / len(shards), high / len(shards))
        factor_of = factor_of * jnp.repeat(jnp.exp(steps), shape[axis_at] // shards_of).reshape((-1,) + (1,) * (len(shape) - 1 - axis_at))
    return factor_of


def gaussian(rng, shape, scale, most, shards=(), kind=jnp.bfloat16):
    result = scale * jax.random.normal(rng, shape, jnp.float32)
    if shards:
        result = result * shard_levels(rng, shape, shards, -0.22, 0.18)
    return jnp.clip(result, -most, most).astype(kind)


def setup_inputs(seed: int = 0) -> dict:
    key_of = jax.random.split(jax.random.key(seed), 4)
    up_blocks = gaussian(key_of[0], (LEVELS, P_SIZE, P_SIZE), 0.2, 1.25, ((0, 128), (2, 4)), jnp.float32)
    level_blocks = draw_level_blocks(jax.random.fold_in(key_of[3], 71), 0)
    down_blocks = gaussian(key_of[2], (LEVELS, P_SIZE, P_SIZE), 0.2, 1.25, ((0, 128), (2, 4)), jnp.float32)
    return {"up_blocks": up_blocks, "level_blocks": level_blocks, "down_blocks": down_blocks}


def sweeps(level_block, up_block, down_block):
    phases = level_block.shape[0]
    out_rates = -jnp.diagonal(level_block)
    inverse = (1.0 / out_rates)[:, None]
    row_index = lax.broadcasted_iota(jnp.int32, (phases, phases), 0)
    col_index = lax.broadcasted_iota(jnp.int32, (phases, phases), 1)
    coupling = jnp.where(row_index == col_index, jnp.float32(0.0), level_block)
    right_side = jnp.concatenate([up_block, down_block], axis=1)
    solution = right_side * inverse
    for sweep_no in range(SWEEPS):
        product = jnp.dot(coupling, solution, precision=lax.Precision.HIGHEST, preferred_element_type=jnp.float32)
        solution = (right_side + product) * inverse
    return solution


def reference(up_blocks, level_blocks, down_blocks):
    top_rate = jnp.max(-jnp.diagonal(level_blocks, axis1=1, axis2=2))
    solved = lax.map(lambda blocks: sweeps(blocks[0], blocks[1], blocks[2]),
                     (level_blocks[1::2], up_blocks[1::2], down_blocks[1::2]))
    solved_below = jnp.concatenate([jnp.zeros((1,) + solved.shape[1:], jnp.float32), solved[:-1]], axis=0)

    def update(blocks):
        level_block, up_block, down_block, above_side, below_side = blocks
        phases = level_block.shape[0]
        upper_terms = jnp.dot(up_block, above_side, precision=lax.Precision.HIGHEST, preferred_element_type=jnp.float32)
        lower_terms = jnp.dot(down_block, below_side, precision=lax.Precision.HIGHEST, preferred_element_type=jnp.float32)
        new_level = (level_block + upper_terms[:, phases:] + lower_terms[:, :phases]) / top_rate
        return new_level, upper_terms[:, :phases] / top_rate, lower_terms[:, phases:] / top_rate

    reduced_level, reduced_up, reduced_down = lax.map(
        update, (level_blocks[0::2], up_blocks[0::2], down_blocks[0::2], solved, solved_below))
    return reduced_level, reduced_up, reduced_down
```

```python
import functools

import jax
import jax.numpy as jnp
from jax import lax
from jax.experimental import pallas as pl
from jax.experimental.pallas import tpu as pltpu
from jax.sharding import PartitionSpec as P

SWEEPS = 2
MESH = pl.DeviceIdType.MESH
F32 = jnp.float32
BF16 = jnp.bfloat16
CHUNKS = 4


def split(x):
    high = x.astype(BF16)
    low = (x - high.astype(F32)).astype(BF16)
    return high, low


def dot(a, b):
    return jnp.dot(a, b, preferred_element_type=F32)


def product(a_high, a_low, x):
    x_high, x_low = split(x)
    return dot(a_high, x_high) + (dot(a_high, x_low) + dot(a_low, x_high))


def kernel(
    sides,
    up,
    level,
    down,
    out_level,
    out_up,
    out_down,
    full,
    high,
    low,
    right,
    mine_even,
    squares,
    solved,
    below,
    upper,
    peaks,
    y_peaks,
    x_peaks,
    z_peaks,
    col_peaks,
    local_sem,
    link_send,
    link_recv,
    relay_send,
    relay_recv,
    own_send,
    own_recv,
    shift_send,
    shift_recv,
    y_send,
    y_recv,
    x_send,
    x_recv,
    z_send,
    z_recv,
    col_send,
    col_recv,
):
    ny, nz, nx = sides
    levels = ny * nz * nx
    lvl = lax.axis_index("lvl")
    col = lax.axis_index("col")
    rows, share = up.shape[1], up.shape[2]
    x = lax.rem(lvl, nx)
    z = lax.rem(lvl // nx, nz)
    y = lvl // (nx * nz)
    partner = col + 1 - 2 * lax.rem(col, 2)
    across = lax.rem(col + 2, 4)

    def at(yy, zz, xx):
        return (yy * nz + zz) * nx + xx

    y_group = [(at(lax.rem(y + j, ny), z, x), col) for j in range(1, ny)]
    x_group = [(at(y, z, lax.rem(x + j, nx)), col) for j in range(1, nx)]
    z_group = [(at(y, lax.rem(z + j, nz), x), col) for j in range(1, nz)]
    col_group = [(lvl, lax.rem(col + j, 4)) for j in range(1, 4)]
    above = lax.rem(lvl + 1, levels)
    beneath = lax.rem(lvl + levels - 1, levels)

    def columns(c):
        return pl.ds(pl.multiple_of(c * share, share), share)

    mine = columns(col)
    theirs = columns(across)
    blocks = (level.at[1], up.at[0], down.at[0])

    local = [
        pltpu.make_async_copy(level.at[0, mine, :], squares.at[0], local_sem.at[0]),
        pltpu.make_async_copy(level.at[1, mine, :], squares.at[1], local_sem.at[1]),
        pltpu.make_async_copy(up.at[1], right.at[:, 0:share], local_sem.at[2]),
        pltpu.make_async_copy(down.at[1], right.at[:, share : 2 * share], local_sem.at[3]),
        pltpu.make_async_copy(level.at[0], mine_even, local_sem.at[4]),
    ] + [
        pltpu.make_async_copy(blocks[m], full.at[m, :, mine], local_sem.at[5 + m]) for m in range(3)
    ]
    for copy in local:
        copy.start()

    barrier = pltpu.get_barrier_semaphore()
    greeted = y_group + x_group + z_group + col_group + [(above, col), (beneath, col)]
    for device in greeted:
        pl.semaphore_signal(barrier, inc=1, device_id=device, device_id_type=MESH)

    local[0].wait()
    local[1].wait()
    row = lax.broadcasted_iota(jnp.int32, (share, share), 0)
    column = lax.broadcasted_iota(jnp.int32, (share, share), 1)
    diagonal = row == column
    rates = jnp.where(diagonal, jnp.maximum(-squares[0], -squares[1]), -jnp.inf)
    peaks[0] = jnp.max(rates.reshape(share // 8, 8, share), axis=0)

    pl.semaphore_wait(barrier, len(greeted))

    def send_peaks(stage, group, slots, send, recv):
        copies = []
        for j, device in enumerate(group):
            copies.append(
                pltpu.make_async_remote_copy(
                    src_ref=peaks.at[stage],
                    dst_ref=slots.at[j],
                    send_sem=send.at[j],
                    recv_sem=recv.at[j],
                    device_id=device,
                    device_id_type=MESH,
                )
            )
            copies[-1].start()
        return copies

    def take_peaks(stage, copies, slots):
        best = peaks[stage]
        for j, copy in enumerate(copies):
            copy.wait_recv()
            best = jnp.maximum(best, slots[j])
        peaks[stage + 1] = best

    step = rows // CHUNKS

    def link(m, i):
        part = pl.ds(i * step, step)
        return pltpu.make_async_remote_copy(
            src_ref=blocks[m].at[part, :],
            dst_ref=full.at[m, part, mine],
            send_sem=link_send.at[m, i],
            recv_sem=link_recv.at[m, i],
            device_id=(lvl, across),
            device_id_type=MESH,
        )

    def relay(m, i):
        part = pl.ds(i * step, step)
        return pltpu.make_async_remote_copy(
            src_ref=full.at[m, part, theirs],
            dst_ref=full.at[m, part, theirs],
            send_sem=relay_send.at[m, i],
            recv_sem=relay_recv.at[m, i],
            device_id=(lvl, partner),
            device_id_type=MESH,
        )

    def own(m):
        return pltpu.make_async_remote_copy(
            src_ref=blocks[m],
            dst_ref=full.at[m, :, mine],
            send_sem=own_send.at[m],
            recv_sem=own_recv.at[m],
            device_id=(lvl, partner),
            device_id_type=MESH,
        )

    col_copies = send_peaks(0, col_group, col_peaks, col_send, col_recv)
    links = [[link(m, i) for i in range(CHUNKS)] for m in range(3)]
    relays = [[relay(m, i) for i in range(CHUNKS)] for m in range(3)]
    owns = [own(m) for m in range(3)]
    for i in range(CHUNKS):
        links[0][i].start()
    owns[0].start()
    for i in range(CHUNKS):
        links[1][i].start()
    owns[1].start()
    take_peaks(0, col_copies, col_peaks)
    y_copies = send_peaks(1, y_group, y_peaks, y_send, y_recv)

    def hand_on(m, i):
        links[m][i].wait_recv()
        relays[m][i].start()

    def gathered(m):
        local[5 + m].wait()
        owns[m].wait_recv()
        for i in range(CHUNKS):
            relays[m][i].wait_recv()

    for i in range(CHUNKS):
        hand_on(0, i)
    take_peaks(1, y_copies, y_peaks)
    x_copies = send_peaks(2, x_group, x_peaks, x_send, x_recv)
    gathered(0)
    local[2].wait()
    local[3].wait()

    inverse = []
    for s in range(rows // share):
        part = slice(s * share, (s + 1) * share)
        square = full[0, part, part]
        inverse.append(1.0 / jnp.sum(jnp.where(diagonal, -square, 0.0), axis=1, keepdims=True))
        high[0, part, :], low[0, part, :] = split(full[0, part, :])
        high[0, part, part], low[0, part, part] = split(jnp.where(diagonal, 0.0, square))
    inverse = jnp.concatenate(inverse, axis=0)
    side = right[...]
    guess = side * inverse
    for _ in range(SWEEPS - 1):
        guess = (side + product(high[0], low[0], guess)) * inverse
    solved[...] = (side + product(high[0], low[0], guess)) * inverse

    shift = pltpu.make_async_remote_copy(
        src_ref=solved,
        dst_ref=below,
        send_sem=shift_send.at[0],
        recv_sem=shift_recv.at[0],
        device_id=(above, col),
        device_id_type=MESH,
    )

    @pl.when(lvl < levels - 1)
    def _():
        shift.start()

    take_peaks(2, x_copies, x_peaks)
    z_copies = send_peaks(3, z_group, z_peaks, z_send, z_recv)
    for i in range(CHUNKS):
        links[2][i].start()
    owns[2].start()
    for i in range(CHUNKS):
        hand_on(1, i)
    gathered(1)
    u_high, u_low = split(full[1])
    upper[...] = product(u_high, u_low, solved[...])

    for i in range(CHUNKS):
        hand_on(2, i)
    gathered(2)
    w_high, w_low = split(full[2])
    high[1] = w_high
    low[1] = w_low
    take_peaks(3, z_copies, z_peaks)
    scale = 1.0 / jnp.max(peaks[4], keepdims=True)[0:1, 0:1]
    local[4].wait()

    @pl.when(lvl > 0)
    def _():
        shift.wait_recv()

    @pl.when(lvl == 0)
    def _():
        below[...] = jnp.zeros_like(below)

    lower = product(high[1], low[1], below[...])
    out_level[0] = (mine_even[...] + upper[:, share:] + lower[:, :share]) * scale
    out_up[0] = upper[:, :share] * scale
    out_down[0] = lower[:, share:] * scale

    for copy in col_copies + y_copies + x_copies + z_copies + owns:
        copy.wait_send()
    for m in range(3):
        for i in range(CHUNKS):
            links[m][i].wait_send()
            relays[m][i].wait_send()

    @pl.when(lvl < levels - 1)
    def _():
        shift.wait_send()


def per_device(sides, up, level, down):
    rows, share = up.shape[1], up.shape[2]
    ny, nz, nx = sides
    block = jax.ShapeDtypeStruct((1, rows, share), F32)
    dma = pltpu.SemaphoreType.DMA
    tile = (8, share)
    return pl.pallas_call(
        functools.partial(kernel, sides),
        out_shape=(block, block, block),
        in_specs=[pl.BlockSpec(memory_space=pl.ANY)] * 3,
        out_specs=(pl.BlockSpec(memory_space=pltpu.VMEM),) * 3,
        scratch_shapes=[
            pltpu.VMEM((3, rows, rows), F32),
            pltpu.VMEM((2, rows, rows), BF16),
            pltpu.VMEM((2, rows, rows), BF16),
            pltpu.VMEM((rows, 2 * share), F32),
            pltpu.VMEM((rows, share), F32),
            pltpu.VMEM((2, share, share), F32),
            pltpu.VMEM((rows, 2 * share), F32),
            pltpu.VMEM((rows, 2 * share), F32),
            pltpu.VMEM((rows, 2 * share), F32),
            pltpu.VMEM((5,) + tile, F32),
            pltpu.VMEM((ny - 1,) + tile, F32),
            pltpu.VMEM((nx - 1,) + tile, F32),
            pltpu.VMEM((nz - 1,) + tile, F32),
            pltpu.VMEM((3,) + tile, F32),
            dma((8,)),
            dma((3, CHUNKS)),
            dma((3, CHUNKS)),
            dma((3, CHUNKS)),
            dma((3, CHUNKS)),
            dma((3,)),
            dma((3,)),
            dma((1,)),
            dma((1,)),
            dma((ny - 1,)),
            dma((ny - 1,)),
            dma((nx - 1,)),
            dma((nx - 1,)),
            dma((nz - 1,)),
            dma((nz - 1,)),
            dma((3,)),
            dma((3,)),
        ],
        compiler_params=pltpu.CompilerParams(
            collective_id=0, has_side_effects=True, vmem_limit_bytes=40 * 1024 * 1024
        ),
    )(up, level, down)


def solution(mesh, sides=(8, 4, 4)):
    placed = P("lvl", None, "col")
    return jax.shard_map(
        functools.partial(per_device, sides),
        mesh=mesh,
        in_specs=(placed, placed, placed),
        out_specs=(placed, placed, placed),
        check_vma=False,
    )
```

```python
import functools

import jax
import jax.numpy as jnp
from jax import lax
from jax.experimental import pallas as pl
from jax.experimental.pallas import tpu as pltpu
from jax.sharding import PartitionSpec as P

SWEEPS = 2
MESH = pl.DeviceIdType.MESH
F32 = jnp.float32
BF16 = jnp.bfloat16
CHUNKS = 4


def split(x):
    high = x.astype(BF16)
    low = (x - high.astype(F32)).astype(BF16)
    return high, low


def dot(a, b):
    return jnp.dot(a, b, preferred_element_type=F32)


def product(a_high, a_low, x):
    x_high, x_low = split(x)
    return dot(a_high, x_high) + (dot(a_high, x_low) + dot(a_low, x_high))


def start_rank(y, ny):
    return jnp.where(y == 0, 0, jnp.where(2 * y <= ny, 2 * y - 1, 2 * (ny - y)))


def kernel(
    sides,
    up,
    level,
    down,
    out_level,
    out_up,
    out_down,
    full,
    high,
    low,
    right,
    mine_even,
    squares,
    solved,
    below,
    hop,
    upper,
    peaks,
    col_peaks,
    x_peaks,
    y_peaks,
    z_peaks,
    local_sem,
    link_send,
    link_recv,
    relay_send,
    relay_recv,
    own_send,
    own_recv,
    shift_send,
    shift_recv,
    hop_send,
    hop_recv,
    forward_send,
    col_send,
    col_recv,
    x_send,
    x_recv,
    y_send,
    y_recv,
    z_send,
    z_recv,
    x_ack,
    y_ack,
    z_ack,
    next_ack,
):
    ny, nz, nx = sides
    lvl = lax.axis_index("lvl")
    col = lax.axis_index("col")
    rows, share = up.shape[1], up.shape[2]
    x = lax.rem(lvl, nx)
    run = lvl // nx
    runs = ny * nz
    z = lax.rem(run, nz)
    y = run // nz
    core = lax.rem(col, 2)
    side = col // 2
    partner = col + 1 - 2 * core
    across = lax.rem(col + 2, 4)

    def at(yy, zz, xx):
        return (yy * nz + zz) * nx + xx

    def signal(semaphore, device):
        pl.semaphore_signal(semaphore, inc=1, device_id=device, device_id_type=MESH)

    rank = start_rank(y, ny)
    x_group = [lax.rem(x + j, nx) for j in range(1, nx)]
    y_group = [lax.rem(y + j, ny) for j in range(1, ny)]
    z_group = [lax.rem(z + j, nz) for j in range(1, nz)]
    x_devices = [(at(y, z, xx), col) for xx in x_group]
    y_devices = [(at(yy, z, x), col) for yy in y_group]
    col_group = [(lvl, lax.rem(col + j, 4)) for j in range(1, 4)]
    head = (run + 1) * nx
    turns = run < runs - 1
    last = x == nx - 1

    def columns(c):
        return pl.ds(pl.multiple_of(c * share, share), share)

    mine = columns(col)
    theirs = columns(across)
    blocks = (level.at[1], up.at[0], down.at[0])

    local = [
        pltpu.make_async_copy(level.at[0, mine, :], squares.at[0], local_sem.at[0]),
        pltpu.make_async_copy(level.at[1, mine, :], squares.at[1], local_sem.at[1]),
        pltpu.make_async_copy(up.at[1], right.at[:, 0:share], local_sem.at[2]),
        pltpu.make_async_copy(down.at[1], right.at[:, share : 2 * share], local_sem.at[3]),
        pltpu.make_async_copy(level.at[0], mine_even, local_sem.at[4]),
    ] + [
        pltpu.make_async_copy(blocks[m], full.at[m, :, mine], local_sem.at[5 + m]) for m in range(3)
    ]

    barrier = pltpu.get_barrier_semaphore()
    for device in col_group:
        signal(barrier, device)
    for copy in local:
        copy.start()
    for xx, device in zip(x_group, x_devices):

        @pl.when(xx > x)
        def _():
            signal(barrier, device)

    for yy, device in zip(y_group, y_devices):

        @pl.when(start_rank(yy, ny) > rank)
        def _():
            signal(barrier, device)

    for zz in z_group:

        @pl.when(zz > z)
        def _():
            for half in range(2):
                signal(barrier, (at(y, zz, x), half * 2 + core))

    @pl.when(turns & (z < nz - 1))
    def _():
        signal(barrier, (head, col))

    @pl.when((x == 0) & (z == 0) & (run > 0))
    def _():
        for xx in range(nx):
            signal(barrier, (lvl - nx + xx, col))

    local[0].wait()
    local[1].wait()
    row = lax.broadcasted_iota(jnp.int32, (share, share), 0)
    column = lax.broadcasted_iota(jnp.int32, (share, share), 1)
    diagonal = row == column
    rates = jnp.where(diagonal, jnp.maximum(-squares[0], -squares[1]), -jnp.inf)
    peaks[0] = jnp.max(rates.reshape(share // 8, 8, share), axis=0)

    expected = 3 + x + rank + 2 * z
    expected = expected + jnp.where((x == 0) & (z > 0), nx, 0)
    expected = expected + jnp.where(turns & (z == nz - 1), 1, 0)
    pl.semaphore_wait(barrier, expected)

    def send_peaks(stage, group, slots, send, recv):
        copies = []
        for j, device in enumerate(group):
            copies.append(
                pltpu.make_async_remote_copy(
                    src_ref=peaks.at[stage],
                    dst_ref=slots.at[j],
                    send_sem=send.at[j],
                    recv_sem=recv.at[j],
                    device_id=device,
                    device_id_type=MESH,
                )
            )
            copies[-1].start()
        return copies

    def take_peaks(stage, copies, slots):
        best = peaks[stage]
        for j, copy in enumerate(copies):
            copy.wait_recv()
            best = jnp.maximum(best, slots[j])
        peaks[stage + 1] = best

    step = rows // CHUNKS

    def link(m, i):
        part = pl.ds(i * step, step)
        return pltpu.make_async_remote_copy(
            src_ref=blocks[m].at[part, :],
            dst_ref=full.at[m, part, mine],
            send_sem=link_send.at[m, i],
            recv_sem=link_recv.at[m, i],
            device_id=(lvl, across),
            device_id_type=MESH,
        )

    def relay(m, i):
        part = pl.ds(i * step, step)
        return pltpu.make_async_remote_copy(
            src_ref=full.at[m, part, theirs],
            dst_ref=full.at[m, part, theirs],
            send_sem=relay_send.at[m, i],
            recv_sem=relay_recv.at[m, i],
            device_id=(lvl, partner),
            device_id_type=MESH,
        )

    def own(m):
        return pltpu.make_async_remote_copy(
            src_ref=blocks[m],
            dst_ref=full.at[m, :, mine],
            send_sem=own_send.at[m],
            recv_sem=own_recv.at[m],
            device_id=(lvl, partner),
            device_id_type=MESH,
        )

    links = [[link(m, i) for i in range(CHUNKS)] for m in range(3)]
    relays = [[relay(m, i) for i in range(CHUNKS)] for m in range(3)]
    owns = [own(m) for m in range(3)]

    col_copies = send_peaks(0, col_group, col_peaks, col_send, col_recv)
    for m in range(3):
        for i in range(CHUNKS):
            links[m][i].start()
        owns[m].start()

    for xx, device in zip(x_group, x_devices):

        @pl.when(xx < x)
        def _():
            signal(x_ack, device)

    for yy, device in zip(y_group, y_devices):

        @pl.when(start_rank(yy, ny) < rank)
        def _():
            signal(y_ack, device)

    for zz in z_group:

        @pl.when(zz < z)
        def _():
            for half in range(2):
                signal(z_ack, (at(y, zz, x), half * 2 + core))

    @pl.when((x == 0) & (z > 0))
    def _():
        for xx in range(nx):
            signal(next_ack, (lvl - nx + xx, col))

    def hand_on(m, i):
        links[m][i].wait_recv()
        relays[m][i].start()

    def gathered(m):
        local[5 + m].wait()
        owns[m].wait_recv()
        for i in range(CHUNKS):
            relays[m][i].wait_recv()

    take_peaks(0, col_copies, col_peaks)

    @pl.when(x < nx - 1)
    def _():
        pl.semaphore_wait(x_ack, nx - 1 - x)

    x_copies = send_peaks(1, x_devices, x_peaks, x_send, x_recv)
    for i in range(CHUNKS):
        hand_on(0, i)
    take_peaks(1, x_copies, x_peaks)

    @pl.when(rank < ny - 1)
    def _():
        pl.semaphore_wait(y_ack, ny - 1 - rank)

    y_copies = send_peaks(2, y_devices, y_peaks, y_send, y_recv)
    gathered(0)
    local[2].wait()
    local[3].wait()

    inverse = []
    for s in range(rows // share):
        part = slice(s * share, (s + 1) * share)
        square = full[0, part, part]
        inverse.append(1.0 / jnp.sum(jnp.where(diagonal, -square, 0.0), axis=1, keepdims=True))
        high[0, part, :], low[0, part, :] = split(full[0, part, :])
        high[0, part, part], low[0, part, part] = split(jnp.where(diagonal, 0.0, square))
    every = jnp.concatenate(inverse, axis=0)
    sides_of = right[...]
    guess = sides_of * every
    for _ in range(SWEEPS - 1):
        guess = (sides_of + product(high[0], low[0], guess)) * every
    guess_high, guess_low = split(guess)

    def piece(q):
        return pl.ds(pl.multiple_of(q * share, share), share)

    def shift(source, q, device):
        return pltpu.make_async_remote_copy(
            src_ref=source,
            dst_ref=below.at[piece(q), :],
            send_sem=shift_send.at[q],
            recv_sem=shift_recv.at[q],
            device_id=(device, col),
            device_id_type=MESH,
        )

    def forward():
        return pltpu.make_async_remote_copy(
            src_ref=hop,
            dst_ref=below.at[piece(x + 1), :],
            send_sem=forward_send.at[0],
            recv_sem=shift_recv.at[x + 1],
            device_id=(head, col),
            device_id_type=MESH,
        )

    def detour(q):
        return pltpu.make_async_remote_copy(
            src_ref=solved.at[piece(q), :],
            dst_ref=hop,
            send_sem=hop_send.at[q - 1],
            recv_sem=hop_recv.at[0],
            device_id=(at(y, z, q - 1), col),
            device_id_type=MESH,
        )

    @pl.when(turns & (z < nz - 1))
    def _():
        pl.semaphore_wait(next_ack, 1)

    pieces = rows // share
    for q in range(pieces):
        part = slice(q * share, (q + 1) * share)
        term = dot(high[0, part, :], guess_high) + (
            dot(high[0, part, :], guess_low) + dot(low[0, part, :], guess_high)
        )
        solved[part, :] = (right[part, :] + term) * inverse[q]

        if q == 0:

            @pl.when(jnp.logical_not(last) | turns)
            def _():
                shift(solved.at[piece(0), :], 0, lvl + 1).start()
        else:

            @pl.when(jnp.logical_not(last))
            def _():
                shift(solved.at[piece(q), :], q, lvl + 1).start()

            @pl.when(last & turns)
            def _():
                detour(q).start()

    take_peaks(2, y_copies, y_peaks)

    @pl.when(z < nz - 1)
    def _():
        pl.semaphore_wait(z_ack, 2 * (nz - 1 - z))


    def z_copy(slot, zz, half, sender):
        return pltpu.make_async_remote_copy(
            src_ref=peaks.at[3],
            dst_ref=z_peaks.at[slot],
            send_sem=z_send.at[sender],
            recv_sem=z_recv.at[slot],
            device_id=(at(y, lax.rem(zz + nz, nz), x), half * 2 + core),
            device_id_type=MESH,
        )

    ahead = [z_copy(slot, z + slot + 1, half, 2 * slot + half) for slot in range(2) for half in range(2)]
    behind = [z_copy(2, z - 1, half, half) for half in range(2)]

    @pl.when(side == 1)
    def _():
        for copy in ahead:
            copy.start()

    @pl.when(side == 0)
    def _():
        for copy in behind:
            copy.start()

    hands_over = jnp.logical_not(last) & turns

    @pl.when(hands_over)
    def _():
        detour(1).wait_recv()
        forward().start()

    for i in range(CHUNKS):
        hand_on(1, i)
    gathered(1)
    u_high, u_low = split(full[1])
    upper[...] = product(u_high, u_low, solved[...])

    for i in range(CHUNKS):
        hand_on(2, i)
    gathered(2)
    w_high, w_low = split(full[2])
    high[1] = w_high
    low[1] = w_low
    local[4].wait()

    @pl.when(lvl == 0)
    def _():
        below[...] = jnp.zeros_like(below)

    lower = 0.0
    for half in range(2):
        part = slice(half * rows // 2, (half + 1) * rows // 2)

        @pl.when(lvl > 0)
        def _():
            for q in range(half * pieces // 2, (half + 1) * pieces // 2):
                shift(solved.at[piece(q), :], q, lvl).wait_recv()

        lower = lower + product(high[1, :, part], low[1, :, part], below[part, :])
    best = peaks[3]
    for slot in range(3):
        z_copy(slot, z, side, 0).wait_recv()
        best = jnp.maximum(best, z_peaks[slot])
    factor = 1.0 / jnp.max(best, keepdims=True)
    out_level[0] = (mine_even[...] + upper[:, share:] + lower[:, :share]) * factor
    out_up[0] = upper[:, :share] * factor
    out_down[0] = lower[:, share:] * factor

    for copy in col_copies + x_copies + y_copies + owns:
        copy.wait_send()
    for m in range(3):
        for i in range(CHUNKS):
            links[m][i].wait_send()
            relays[m][i].wait_send()

    @pl.when(side == 1)
    def _():
        for copy in ahead:
            copy.wait_send()

    @pl.when(side == 0)
    def _():
        for copy in behind:
            copy.wait_send()

    @pl.when(jnp.logical_not(last) | turns)
    def _():
        shift(solved.at[piece(0), :], 0, lvl).wait_send()

    @pl.when(jnp.logical_not(last))
    def _():
        for q in range(1, pieces):
            shift(solved.at[piece(q), :], q, lvl).wait_send()

    @pl.when(last & turns)
    def _():
        for q in range(1, pieces):
            detour(q).wait_send()

    @pl.when(hands_over)
    def _():
        forward().wait_send()


def per_device(sides, up, level, down):
    rows, share = up.shape[1], up.shape[2]
    ny, nz, nx = sides
    dma = pltpu.SemaphoreType.DMA
    regular = pltpu.SemaphoreType.REGULAR
    tile = (8, share)
    block = jax.ShapeDtypeStruct((1, rows, share), F32)
    return pl.pallas_call(
        functools.partial(kernel, sides),
        out_shape=(block, block, block),
        in_specs=[pl.BlockSpec(memory_space=pl.ANY)] * 3,
        out_specs=(pl.BlockSpec(memory_space=pltpu.VMEM),) * 3,
        scratch_shapes=[
            pltpu.VMEM((3, rows, rows), F32),
            pltpu.VMEM((2, rows, rows), BF16),
            pltpu.VMEM((2, rows, rows), BF16),
            pltpu.VMEM((rows, 2 * share), F32),
            pltpu.VMEM((rows, share), F32),
            pltpu.VMEM((2, share, share), F32),
            pltpu.VMEM((rows, 2 * share), F32),
            pltpu.VMEM((rows, 2 * share), F32),
            pltpu.VMEM((share, 2 * share), F32),
            pltpu.VMEM((rows, 2 * share), F32),
            pltpu.VMEM((4,) + tile, F32),
            pltpu.VMEM((3,) + tile, F32),
            pltpu.VMEM((nx - 1,) + tile, F32),
            pltpu.VMEM((ny - 1,) + tile, F32),
            pltpu.VMEM((3,) + tile, F32),
            dma((8,)),
            dma((3, CHUNKS)),
            dma((3, CHUNKS)),
            dma((3, CHUNKS)),
            dma((3, CHUNKS)),
            dma((3,)),
            dma((3,)),
            dma((rows // share,)),
            dma((rows // share,)),
            dma((nx - 1,)),
            dma((1,)),
            dma((1,)),
            dma((3,)),
            dma((3,)),
            dma((nx - 1,)),
            dma((nx - 1,)),
            dma((ny - 1,)),
            dma((ny - 1,)),
            dma((4,)),
            dma((3,)),
            regular,
            regular,
            regular,
            regular,
        ],
        compiler_params=pltpu.CompilerParams(
            collective_id=0, has_side_effects=True, vmem_limit_bytes=62 * 1024 * 1024
        ),
    )(up, level, down)


def solution(mesh, sides=(8, 4, 4)):
    placed = P("lvl", None, "col")
    return jax.shard_map(
        functools.partial(per_device, sides),
        mesh=mesh,
        in_specs=(placed, placed, placed),
        out_specs=(placed, placed, placed),
        check_vma=False,
    )
```

```python
import functools

import jax
import jax.numpy as jnp
from jax import lax
from jax.experimental import pallas as pl
from jax.experimental.pallas import tpu as pltpu
from jax.sharding import PartitionSpec as P

SWEEPS = 2
MESH = pl.DeviceIdType.MESH
F32 = jnp.float32
BF16 = jnp.bfloat16
CHUNKS = 4
EARLY = 1
UNIT = 64
STRAIGHT = -1
LATE_ROUTES = (-1, -1, -1, -1, 0, 0, 2, 2)


def slot_of(u):
    return sum(LATE_ROUTES[v] == LATE_ROUTES[u] for v in range(u))


def split(x):
    high = x.astype(BF16)
    low = (x - high.astype(F32)).astype(BF16)
    return high, low


def dot(a, b):
    return jnp.dot(a, b, preferred_element_type=F32)


def product(a_high, a_low, x):
    x_high, x_low = split(x)
    return dot(a_high, x_high) + (dot(a_high, x_low) + dot(a_low, x_high))


def start_rank(y, ny, first_last):
    rank = jnp.where(y == 0, 0, jnp.where(2 * y <= ny, 2 * y - 1, 2 * (ny - y)))
    return jnp.where(first_last, jnp.where(y == 0, ny - 1, rank - 1), rank)


def x_rank(x, nx, first_last):
    return jnp.where(first_last, jnp.where(x == 0, nx - 1, x - 1), x)


def kernel(
    sides,
    up,
    level,
    down,
    out_level,
    out_up,
    out_down,
    full,
    high,
    low,
    right,
    mine_even,
    squares,
    solved,
    below,
    hop,
    upper,
    peaks,
    col_peaks,
    x_peaks,
    y_peaks,
    z_peaks,
    local_sem,
    link_send,
    link_recv,
    relay_send,
    relay_recv,
    own_send,
    own_recv,
    shift_send,
    shift_recv,
    hop_recv,
    forward_send,
    col_send,
    col_recv,
    x_send,
    x_recv,
    y_send,
    y_recv,
    z_send,
    z_recv,
    x_ack,
    y_ack,
    z_ack,
    next_ack,
):
    ny, nz, nx = sides
    lvl = lax.axis_index("lvl")
    col = lax.axis_index("col")
    rows, share = up.shape[1], up.shape[2]
    x = lax.rem(lvl, nx)
    run = lvl // nx
    runs = ny * nz
    z = lax.rem(run, nz)
    y = run // nz
    core = lax.rem(col, 2)
    side = col // 2
    partner = col + 1 - 2 * core
    across = lax.rem(col + 2, 4)

    def at(yy, zz, xx):
        return (yy * nz + zz) * nx + xx

    def signal(semaphore, device):
        pl.semaphore_signal(semaphore, inc=1, device_id=device, device_id_type=MESH)

    y_late = (x == 0) & (z == 0) & (col == 0)
    x_late = (y == 0) & (z == 0) & (col == 0)
    rank = start_rank(y, ny, y_late)
    place = x_rank(x, nx, x_late)
    x_group = [lax.rem(x + j, nx) for j in range(1, nx)]
    y_group = [lax.rem(y + j, ny) for j in range(1, ny)]
    z_group = [lax.rem(z + j, nz) for j in range(1, nz)]
    x_devices = [(at(y, z, xx), col) for xx in x_group]
    y_devices = [(at(yy, z, x), col) for yy in y_group]
    col_group = [(lvl, lax.rem(col + j, 4)) for j in range(1, 4)]
    head = (run + 1) * nx
    turns = run < runs - 1
    last = x == nx - 1
    holds = (z == nz - 1) & turns & ((x != 1) | (1 in LATE_ROUTES))

    def columns(c):
        return pl.ds(pl.multiple_of(c * share, share), share)

    mine = columns(col)
    theirs = columns(across)
    blocks = (level.at[1], up.at[0], down.at[0])

    local = [
        pltpu.make_async_copy(level.at[0, mine, :], squares.at[0], local_sem.at[0]),
        pltpu.make_async_copy(level.at[1, mine, :], squares.at[1], local_sem.at[1]),
        pltpu.make_async_copy(up.at[1], right.at[:, 0:share], local_sem.at[2]),
        pltpu.make_async_copy(down.at[1], right.at[:, share : 2 * share], local_sem.at[3]),
        pltpu.make_async_copy(level.at[0], mine_even, local_sem.at[4]),
    ] + [
        pltpu.make_async_copy(blocks[m], full.at[m, :, mine], local_sem.at[5 + m]) for m in range(3)
    ]

    barrier = pltpu.get_barrier_semaphore()
    for device in col_group:
        signal(barrier, device)
    for copy in local:
        copy.start()
    for xx, device in zip(x_group, x_devices):

        @pl.when(x_rank(xx, nx, x_late) > place)
        def _():
            signal(barrier, device)

    for yy, device in zip(y_group, y_devices):

        @pl.when(start_rank(yy, ny, y_late) > rank)
        def _():
            signal(barrier, device)

    for zz in z_group:

        @pl.when(zz > z)
        def _():
            for half in range(2):
                signal(barrier, (at(y, zz, x), half * 2 + core))

    @pl.when(turns & (z < nz - 1))
    def _():
        signal(barrier, (head, col))

    @pl.when((x == 0) & (z == 0) & (run > 0))
    def _():
        for xx in range(nx):
            signal(barrier, (lvl - nx + xx, col))

    local[0].wait()
    local[1].wait()
    row = lax.broadcasted_iota(jnp.int32, (share, share), 0)
    column = lax.broadcasted_iota(jnp.int32, (share, share), 1)
    diagonal = row == column
    rates = jnp.where(diagonal, jnp.maximum(-squares[0], -squares[1]), -jnp.inf)
    peaks[0] = jnp.max(rates.reshape(share // 8, 8, share), axis=0)

    expected = 3 + place + rank + 2 * z
    expected = expected + jnp.where((x == 0) & (z > 0), nx, 0)
    expected = expected + jnp.where(turns & (z == nz - 1), 1, 0)
    pl.semaphore_wait(barrier, expected)

    def send_peaks(stage, group, slots, send, recv):
        copies = []
        for j, device in enumerate(group):
            copies.append(
                pltpu.make_async_remote_copy(
                    src_ref=peaks.at[stage],
                    dst_ref=slots.at[j],
                    send_sem=send.at[j],
                    recv_sem=recv.at[j],
                    device_id=device,
                    device_id_type=MESH,
                )
            )
            copies[-1].start()
        return copies

    def take_peaks(stage, copies, slots):
        best = peaks[stage]
        for j, copy in enumerate(copies):
            copy.wait_recv()
            best = jnp.maximum(best, slots[j])
        peaks[stage + 1] = best

    step = rows // CHUNKS

    def link(m, i):
        part = pl.ds(i * step, step)
        return pltpu.make_async_remote_copy(
            src_ref=blocks[m].at[part, :],
            dst_ref=full.at[m, part, mine],
            send_sem=link_send.at[m, i],
            recv_sem=link_recv.at[m, i],
            device_id=(lvl, across),
            device_id_type=MESH,
        )

    def relay(m, i):
        part = pl.ds(i * step, step)
        return pltpu.make_async_remote_copy(
            src_ref=full.at[m, part, theirs],
            dst_ref=full.at[m, part, theirs],
            send_sem=relay_send.at[m, i],
            recv_sem=relay_recv.at[m, i],
            device_id=(lvl, partner),
            device_id_type=MESH,
        )

    def own(m):
        return pltpu.make_async_remote_copy(
            src_ref=blocks[m],
            dst_ref=full.at[m, :, mine],
            send_sem=own_send.at[m],
            recv_sem=own_recv.at[m],
            device_id=(lvl, partner),
            device_id_type=MESH,
        )

    links = [[link(m, i) for i in range(CHUNKS)] for m in range(3)]
    relays = [[relay(m, i) for i in range(CHUNKS)] for m in range(3)]
    owns = [own(m) for m in range(3)]

    col_copies = send_peaks(0, col_group, col_peaks, col_send, col_recv)
    for m in range(3):
        for i in range(CHUNKS if m < 2 else EARLY):
            links[m][i].start()
        owns[m].start()

    @pl.when(jnp.logical_not(holds))
    def _():
        for i in range(EARLY, CHUNKS):
            links[2][i].start()

    for xx, device in zip(x_group, x_devices):

        @pl.when(x_rank(xx, nx, x_late) < place)
        def _():
            signal(x_ack, device)

    for yy, device in zip(y_group, y_devices):

        @pl.when(start_rank(yy, ny, y_late) < rank)
        def _():
            signal(y_ack, device)

    for zz in z_group:

        @pl.when(zz < z)
        def _():
            for half in range(2):
                signal(z_ack, (at(y, zz, x), half * 2 + core))

    @pl.when((x == 0) & (z > 0))
    def _():
        for xx in range(nx):
            signal(next_ack, (lvl - nx + xx, col))

    def hand_on(m, i):
        links[m][i].wait_recv()
        relays[m][i].start()

    def gathered(m):
        local[5 + m].wait()
        owns[m].wait_recv()
        for i in range(CHUNKS):
            relays[m][i].wait_recv()

    take_peaks(0, col_copies, col_peaks)

    @pl.when(place < nx - 1)
    def _():
        pl.semaphore_wait(x_ack, nx - 1 - place)

    x_copies = send_peaks(1, x_devices, x_peaks, x_send, x_recv)
    for i in range(CHUNKS):
        hand_on(0, i)
    take_peaks(1, x_copies, x_peaks)

    @pl.when(rank < ny - 1)
    def _():
        pl.semaphore_wait(y_ack, ny - 1 - rank)

    y_copies = send_peaks(2, y_devices, y_peaks, y_send, y_recv)
    gathered(0)
    local[2].wait()
    local[3].wait()

    inverse = []
    for s in range(rows // share):
        part = slice(s * share, (s + 1) * share)
        square = full[0, part, part]
        inverse.append(1.0 / jnp.sum(jnp.where(diagonal, -square, 0.0), axis=1, keepdims=True))
        high[0, part, :], low[0, part, :] = split(full[0, part, :])
        high[0, part, part], low[0, part, part] = split(jnp.where(diagonal, 0.0, square))
    every = jnp.concatenate(inverse, axis=0)
    sides_of = right[...]
    guess = sides_of * every
    for _ in range(SWEEPS - 1):
        guess = (sides_of + product(high[0], low[0], guess)) * every
    guess_high, guess_low = split(guess)

    units = rows // UNIT
    per_piece = units // (rows // share)

    def unit(u):
        return slice(u * UNIT, (u + 1) * UNIT)

    def shift(u, device):
        return pltpu.make_async_remote_copy(
            src_ref=solved.at[unit(u), :],
            dst_ref=below.at[unit(u), :],
            send_sem=shift_send.at[u],
            recv_sem=shift_recv.at[u],
            device_id=(device, col),
            device_id_type=MESH,
        )

    def detour(u, target, slot):
        return pltpu.make_async_remote_copy(
            src_ref=solved.at[unit(u), :],
            dst_ref=hop.at[slot],
            send_sem=shift_send.at[u],
            recv_sem=hop_recv.at[slot],
            device_id=(at(y, z, target), col),
            device_id_type=MESH,
        )

    def forward(slot, u):
        return pltpu.make_async_remote_copy(
            src_ref=hop.at[slot],
            dst_ref=below.at[pl.ds(pl.multiple_of(u * UNIT, UNIT), UNIT), :],
            send_sem=forward_send.at[slot],
            recv_sem=shift_recv.at[u],
            device_id=(head, col),
            device_id_type=MESH,
        )

    @pl.when(turns & (z < nz - 1))
    def _():
        pl.semaphore_wait(next_ack, 1)

    pieces = rows // share
    for q in reversed(range(pieces)):
        part = slice(q * share, (q + 1) * share)
        term = dot(high[0, part, :], guess_high) + (
            dot(high[0, part, :], guess_low) + dot(low[0, part, :], guess_high)
        )
        solved[part, :] = (right[part, :] + term) * inverse[q]

        mine_of = [u for u in reversed(range(units)) if u * UNIT // share == q]

        @pl.when(jnp.logical_not(last))
        def _():
            for u in mine_of:
                shift(u, lvl + 1).start()

        @pl.when(last & turns & (z < nz - 1))
        def _():
            for u in mine_of:
                (detour(u, q - 1, u % per_piece) if q else shift(u, lvl + 1)).start()

        @pl.when(last & turns & (z == nz - 1))
        def _():
            for u in mine_of:
                route = LATE_ROUTES[u]
                (shift(u, lvl + 1) if route == STRAIGHT else detour(u, route, slot_of(u))).start()

    take_peaks(2, y_copies, y_peaks)

    @pl.when(z < nz - 1)
    def _():
        pl.semaphore_wait(z_ack, 2 * (nz - 1 - z))


    def z_copy(slot, zz, half, sender):
        return pltpu.make_async_remote_copy(
            src_ref=peaks.at[3],
            dst_ref=z_peaks.at[slot],
            send_sem=z_send.at[sender],
            recv_sem=z_recv.at[slot],
            device_id=(at(y, lax.rem(zz + nz, nz), x), half * 2 + core),
            device_id_type=MESH,
        )

    ahead = [z_copy(slot, z + slot + 1, half, 2 * slot + half) for slot in range(2) for half in range(2)]
    behind = [z_copy(2, z - 1, half, half) for half in range(2)]

    @pl.when(side == 1)
    def _():
        for copy in ahead:
            copy.start()

    @pl.when(side == 0)
    def _():
        for copy in behind:
            copy.start()

    def rest():
        for i in range(EARLY, CHUNKS):
            links[2][i].start()

    @pl.when(holds & last)
    def _():
        rest()

    def hand_over(act):
        @pl.when((z < nz - 1) & jnp.logical_not(last))
        def _():
            for slot in reversed(range(per_piece)):
                act(slot, forward(slot, per_piece * (x + 1) + slot))

        for route in sorted(set(LATE_ROUTES) - {STRAIGHT}):

            @pl.when((z == nz - 1) & (x == route) & turns)
            def _():
                for u in reversed(range(units)):
                    if LATE_ROUTES[u] == route:
                        act(slot_of(u), forward(slot_of(u), u))

    def take_and_start(slot, copy):
        detour(0, 0, slot).wait_recv()
        copy.start()

    hand_over(take_and_start)

    @pl.when(holds & jnp.logical_not(last))
    def _():
        rest()

    for i in range(CHUNKS):
        hand_on(1, i)
    gathered(1)
    u_high, u_low = split(full[1])
    upper[...] = product(u_high, u_low, solved[...])

    for i in range(CHUNKS):
        hand_on(2, i)
    gathered(2)
    w_high, w_low = split(full[2])
    high[1] = w_high
    low[1] = w_low
    local[4].wait()

    @pl.when(lvl == 0)
    def _():
        below[...] = jnp.zeros_like(below)

    best = peaks[3]
    for slot in range(3):
        z_copy(slot, z, side, 0).wait_recv()
        best = jnp.maximum(best, z_peaks[slot])
    factor = 1.0 / jnp.max(best, keepdims=True)
    out_level[0] = (mine_even[...] + upper[:, share:]) * factor
    out_up[0] = upper[:, :share] * factor

    lower = 0.0
    for q in reversed(range(pieces)):
        part = slice(q * share, (q + 1) * share)

        @pl.when(lvl > 0)
        def _():
            for u in range(q * per_piece, (q + 1) * per_piece):
                shift(u, lvl).wait_recv()

        lower = lower + product(high[1, :, part], low[1, :, part], below[part, :])
    out_level[0] = out_level[0] + lower[:, :share] * factor
    out_down[0] = lower[:, share:] * factor

    for copy in col_copies + x_copies + y_copies + owns:
        copy.wait_send()
    for m in range(3):
        for i in range(CHUNKS):
            links[m][i].wait_send()
            relays[m][i].wait_send()

    @pl.when(side == 1)
    def _():
        for copy in ahead:
            copy.wait_send()

    @pl.when(side == 0)
    def _():
        for copy in behind:
            copy.wait_send()

    @pl.when(jnp.logical_not(last) | turns)
    def _():
        for u in range(units):
            shift(u, lvl).wait_send()

    hand_over(lambda slot, copy: copy.wait_send())


def place_results(level, up, down, out_level, out_up, out_down, sem):
    copies = [
        pltpu.make_async_copy(source, target, sem.at[i])
        for i, (source, target) in enumerate(((level, out_level), (up, out_up), (down, out_down)))
    ]
    for copy in copies:
        copy.start()
    for copy in copies:
        copy.wait()


def per_device(sides, up, level, down):
    rows, share = up.shape[1], up.shape[2]
    ny, nz, nx = sides
    dma = pltpu.SemaphoreType.DMA
    regular = pltpu.SemaphoreType.REGULAR
    tile = (8, share)
    block = jax.ShapeDtypeStruct((1, rows, share), F32)
    results = pl.pallas_call(
        functools.partial(kernel, sides),
        out_shape=(block, block, block),
        in_specs=[pl.BlockSpec(memory_space=pl.ANY)] * 3,
        out_specs=(pl.BlockSpec(memory_space=pltpu.VMEM),) * 3,
        scratch_shapes=[
            pltpu.VMEM((3, rows, rows), F32),
            pltpu.VMEM((2, rows, rows), BF16),
            pltpu.VMEM((2, rows, rows), BF16),
            pltpu.VMEM((rows, 2 * share), F32),
            pltpu.VMEM((rows, share), F32),
            pltpu.VMEM((2, share, share), F32),
            pltpu.VMEM((rows, 2 * share), F32),
            pltpu.VMEM((rows, 2 * share), F32),
            pltpu.VMEM((rows // UNIT // 2, UNIT, 2 * share), F32),
            pltpu.VMEM((rows, 2 * share), F32),
            pltpu.VMEM((4,) + tile, F32),
            pltpu.VMEM((3,) + tile, F32),
            pltpu.VMEM((nx - 1,) + tile, F32),
            pltpu.VMEM((ny - 1,) + tile, F32),
            pltpu.VMEM((3,) + tile, F32),
            dma((8,)),
            dma((3, CHUNKS)),
            dma((3, CHUNKS)),
            dma((3, CHUNKS)),
            dma((3, CHUNKS)),
            dma((3,)),
            dma((3,)),
            dma((rows // UNIT,)),
            dma((rows // UNIT,)),
            dma((rows // UNIT // 2,)),
            dma((rows // UNIT // 2,)),
            dma((3,)),
            dma((3,)),
            dma((nx - 1,)),
            dma((nx - 1,)),
            dma((ny - 1,)),
            dma((ny - 1,)),
            dma((4,)),
            dma((3,)),
            regular,
            regular,
            regular,
            regular,
        ],
        compiler_params=pltpu.CompilerParams(
            collective_id=0, has_side_effects=True, vmem_limit_bytes=40 * 1024 * 1024
        ),
    )(*(pltpu.with_memory_space_constraint(v, pltpu.HBM) for v in (up, level, down)))
    return pl.pallas_call(
        place_results,
        out_shape=(block, block, block),
        in_specs=[pl.BlockSpec(memory_space=pltpu.VMEM)] * 3,
        out_specs=(pl.BlockSpec(memory_space=pl.ANY),) * 3,
        scratch_shapes=[dma((3,))],
        compiler_params=pltpu.CompilerParams(vmem_limit_bytes=8 * 1024 * 1024),
    )(*results)


def solution(mesh, sides=(8, 4, 4)):
    placed = P("lvl", None, "col")
    return jax.shard_map(
        functools.partial(per_device, sides),
        mesh=mesh,
        in_specs=(placed, placed, placed),
        out_specs=(placed, placed, placed),
        check_vma=False,
    )
```

```python
import functools

import jax
import jax.numpy as jnp
from jax import lax
from jax.experimental import pallas as pl
from jax.experimental.pallas import tpu as pltpu
from jax.sharding import PartitionSpec as P

SWEEPS = 2
MESH = pl.DeviceIdType.MESH
F32 = jnp.float32
BF16 = jnp.bfloat16
CHUNKS = 4
EARLY = 1
UNIT = 64
STRAIGHT = -1
LATE_ROUTES = (-1, -1, -1, 0, 0, 0, 2, 2)


def slot_of(u):
    return sum(LATE_ROUTES[v] == LATE_ROUTES[u] for v in range(u))


def split(x):
    high = x.astype(BF16)
    low = (x - high.astype(F32)).astype(BF16)
    return high, low


def dot(a, b):
    return jnp.dot(a, b, preferred_element_type=F32)


def product(a_high, a_low, x):
    x_high, x_low = split(x)
    return dot(a_high, x_high) + (dot(a_high, x_low) + dot(a_low, x_high))


def start_rank(y, ny, first_last):
    rank = jnp.where(y == 0, 0, jnp.where(2 * y <= ny, 2 * y - 1, 2 * (ny - y)))
    return jnp.where(first_last, jnp.where(y == 0, ny - 1, rank - 1), rank)


def x_rank(x, nx, first_last):
    return jnp.where(first_last, jnp.where(x == 0, nx - 1, x - 1), x)


def kernel(
    sides,
    up,
    level,
    down,
    out_level,
    out_up,
    out_down,
    full,
    high,
    low,
    right,
    mine_even,
    squares,
    solved,
    below,
    hop,
    upper,
    peaks,
    col_peaks,
    x_peaks,
    y_peaks,
    z_peaks,
    local_sem,
    link_send,
    link_recv,
    relay_send,
    relay_recv,
    own_send,
    own_recv,
    shift_send,
    shift_recv,
    hop_recv,
    forward_send,
    col_send,
    col_recv,
    x_send,
    x_recv,
    y_send,
    y_recv,
    z_send,
    z_recv,
    x_ack,
    y_ack,
    z_ack,
    next_ack,
):
    ny, nz, nx = sides
    lvl = lax.axis_index("lvl")
    col = lax.axis_index("col")
    rows, share = up.shape[1], up.shape[2]
    x = lax.rem(lvl, nx)
    run = lvl // nx
    runs = ny * nz
    z = lax.rem(run, nz)
    y = run // nz
    core = lax.rem(col, 2)
    side = col // 2
    partner = col + 1 - 2 * core
    across = lax.rem(col + 2, 4)

    def at(yy, zz, xx):
        return (yy * nz + zz) * nx + xx

    def signal(semaphore, device):
        pl.semaphore_signal(semaphore, inc=1, device_id=device, device_id_type=MESH)

    y_late = (x == 0) & (z == 0) & (col == 0)
    x_late = (y == 0) & (z == 0) & (col == 0)
    rank = start_rank(y, ny, y_late)
    place = x_rank(x, nx, x_late)
    x_group = [lax.rem(x + j, nx) for j in range(1, nx)]
    y_group = [lax.rem(y + j, ny) for j in range(1, ny)]
    z_group = [lax.rem(z + j, nz) for j in range(1, nz)]
    x_devices = [(at(y, z, xx), col) for xx in x_group]
    y_devices = [(at(yy, z, x), col) for yy in y_group]
    col_group = [(lvl, lax.rem(col + j, 4)) for j in range(1, 4)]
    head = (run + 1) * nx
    turns = run < runs - 1
    last = x == nx - 1
    holds = (z == nz - 1) & turns & ((x != 1) | (1 in LATE_ROUTES))

    def columns(c):
        return pl.ds(pl.multiple_of(c * share, share), share)

    mine = columns(col)
    theirs = columns(across)
    blocks = (level.at[1], up.at[0], down.at[0])

    local = [
        pltpu.make_async_copy(level.at[0, mine, :], squares.at[0], local_sem.at[0]),
        pltpu.make_async_copy(level.at[1, mine, :], squares.at[1], local_sem.at[1]),
        pltpu.make_async_copy(up.at[1], right.at[:, 0:share], local_sem.at[2]),
        pltpu.make_async_copy(down.at[1], right.at[:, share : 2 * share], local_sem.at[3]),
        pltpu.make_async_copy(level.at[0], mine_even, local_sem.at[4]),
    ] + [
        pltpu.make_async_copy(blocks[m], full.at[m, :, mine], local_sem.at[5 + m]) for m in range(3)
    ]

    barrier = pltpu.get_barrier_semaphore()
    for device in col_group:
        signal(barrier, device)
    for copy in local:
        copy.start()
    for xx, device in zip(x_group, x_devices):

        @pl.when(x_rank(xx, nx, x_late) > place)
        def _():
            signal(barrier, device)

    for yy, device in zip(y_group, y_devices):

        @pl.when(start_rank(yy, ny, y_late) > rank)
        def _():
            signal(barrier, device)

    for zz in z_group:

        @pl.when(zz > z)
        def _():
            for half in range(2):
                signal(barrier, (at(y, zz, x), half * 2 + core))

    @pl.when(turns & (z < nz - 1))
    def _():
        signal(barrier, (head, col))

    @pl.when((x == 0) & (z == 0) & (run > 0))
    def _():
        for xx in range(nx):
            signal(barrier, (lvl - nx + xx, col))

    local[0].wait()
    local[1].wait()
    row = lax.broadcasted_iota(jnp.int32, (share, share), 0)
    column = lax.broadcasted_iota(jnp.int32, (share, share), 1)
    diagonal = row == column
    rates = jnp.where(diagonal, jnp.maximum(-squares[0], -squares[1]), -jnp.inf)
    peaks[0] = jnp.max(rates.reshape(share // 8, 8, share), axis=0)

    expected = 3 + place + rank + 2 * z
    expected = expected + jnp.where((x == 0) & (z > 0), nx, 0)
    expected = expected + jnp.where(turns & (z == nz - 1), 1, 0)
    pl.semaphore_wait(barrier, expected)

    def send_peaks(stage, group, slots, send, recv):
        copies = []
        for j, device in enumerate(group):
            copies.append(
                pltpu.make_async_remote_copy(
                    src_ref=peaks.at[stage],
                    dst_ref=slots.at[j],
                    send_sem=send.at[j],
                    recv_sem=recv.at[j],
                    device_id=device,
                    device_id_type=MESH,
                )
            )
            copies[-1].start()
        return copies

    def take_peaks(stage, copies, slots):
        best = peaks[stage]
        for j, copy in enumerate(copies):
            copy.wait_recv()
            best = jnp.maximum(best, slots[j])
        peaks[stage + 1] = best

    step = rows // CHUNKS

    def link(m, i):
        part = pl.ds(i * step, step)
        return pltpu.make_async_remote_copy(
            src_ref=blocks[m].at[part, :],
            dst_ref=full.at[m, part, mine],
            send_sem=link_send.at[m, i],
            recv_sem=link_recv.at[m, i],
            device_id=(lvl, across),
            device_id_type=MESH,
        )

    def relay(m, i):
        part = pl.ds(i * step, step)
        return pltpu.make_async_remote_copy(
            src_ref=full.at[m, part, theirs],
            dst_ref=full.at[m, part, theirs],
            send_sem=relay_send.at[m, i],
            recv_sem=relay_recv.at[m, i],
            device_id=(lvl, partner),
            device_id_type=MESH,
        )

    def own(m):
        return pltpu.make_async_remote_copy(
            src_ref=blocks[m],
            dst_ref=full.at[m, :, mine],
            send_sem=own_send.at[m],
            recv_sem=own_recv.at[m],
            device_id=(lvl, partner),
            device_id_type=MESH,
        )

    links = [[link(m, i) for i in range(CHUNKS)] for m in range(3)]
    relays = [[relay(m, i) for i in range(CHUNKS)] for m in range(3)]
    owns = [own(m) for m in range(3)]

    col_copies = send_peaks(0, col_group, col_peaks, col_send, col_recv)
    for i in range(CHUNKS):
        links[0][i].start()
    for m in range(3):
        owns[m].start()

    for xx, device in zip(x_group, x_devices):

        @pl.when(x_rank(xx, nx, x_late) < place)
        def _():
            signal(x_ack, device)

    for yy, device in zip(y_group, y_devices):

        @pl.when(start_rank(yy, ny, y_late) < rank)
        def _():
            signal(y_ack, device)

    for zz in z_group:

        @pl.when(zz < z)
        def _():
            for half in range(2):
                signal(z_ack, (at(y, zz, x), half * 2 + core))

    @pl.when((x == 0) & (z > 0))
    def _():
        for xx in range(nx):
            signal(next_ack, (lvl - nx + xx, col))

    def hand_on(m, i):
        links[m][i].wait_recv()
        relays[m][i].start()

    def gathered(m):
        local[5 + m].wait()
        owns[m].wait_recv()
        for i in range(CHUNKS):
            relays[m][i].wait_recv()

    take_peaks(0, col_copies, col_peaks)

    @pl.when(place < nx - 1)
    def _():
        pl.semaphore_wait(x_ack, nx - 1 - place)

    x_copies = send_peaks(1, x_devices, x_peaks, x_send, x_recv)
    for i in range(CHUNKS - 1):
        hand_on(0, i)
    for i in range(CHUNKS):
        links[1][i].start()
    hand_on(0, CHUNKS - 1)
    take_peaks(1, x_copies, x_peaks)

    @pl.when(rank < ny - 1)
    def _():
        pl.semaphore_wait(y_ack, ny - 1 - rank)

    y_copies = send_peaks(2, y_devices, y_peaks, y_send, y_recv)
    gathered(0)
    local[2].wait()
    local[3].wait()
    for i in range(EARLY):
        links[2][i].start()

    @pl.when(jnp.logical_not(holds))
    def _():
        for i in range(EARLY, CHUNKS):
            links[2][i].start()

    inverse = []
    for s in range(rows // share):
        part = slice(s * share, (s + 1) * share)
        square = full[0, part, part]
        inverse.append(1.0 / jnp.sum(jnp.where(diagonal, -square, 0.0), axis=1, keepdims=True))
        high[0, part, :], low[0, part, :] = split(full[0, part, :])
        high[0, part, part], low[0, part, part] = split(jnp.where(diagonal, 0.0, square))
    every = jnp.concatenate(inverse, axis=0)
    sides_of = right[...]
    guess = sides_of * every
    for _ in range(SWEEPS - 1):
        guess = (sides_of + product(high[0], low[0], guess)) * every
    guess_high, guess_low = split(guess)

    units = rows // UNIT
    per_piece = units // (rows // share)

    def unit(u):
        return slice(u * UNIT, (u + 1) * UNIT)

    def shift(u, device):
        return pltpu.make_async_remote_copy(
            src_ref=solved.at[unit(u), :],
            dst_ref=below.at[unit(u), :],
            send_sem=shift_send.at[u],
            recv_sem=shift_recv.at[u],
            device_id=(device, col),
            device_id_type=MESH,
        )

    def detour(u, target, slot):
        return pltpu.make_async_remote_copy(
            src_ref=solved.at[unit(u), :],
            dst_ref=hop.at[slot],
            send_sem=shift_send.at[u],
            recv_sem=hop_recv.at[slot],
            device_id=(at(y, z, target), col),
            device_id_type=MESH,
        )

    def forward(slot, u):
        return pltpu.make_async_remote_copy(
            src_ref=hop.at[slot],
            dst_ref=below.at[pl.ds(pl.multiple_of(u * UNIT, UNIT), UNIT), :],
            send_sem=forward_send.at[slot],
            recv_sem=shift_recv.at[u],
            device_id=(head, col),
            device_id_type=MESH,
        )

    @pl.when(turns & (z < nz - 1))
    def _():
        pl.semaphore_wait(next_ack, 1)

    pieces = rows // share
    for q in reversed(range(pieces)):
        part = slice(q * share, (q + 1) * share)
        term = dot(high[0, part, :], guess_high) + (
            dot(high[0, part, :], guess_low) + dot(low[0, part, :], guess_high)
        )
        solved[part, :] = (right[part, :] + term) * inverse[q]

        mine_of = [u for u in reversed(range(units)) if u * UNIT // share == q]

        @pl.when(jnp.logical_not(last))
        def _():
            for u in mine_of:
                shift(u, lvl + 1).start()

        if q > 0:

            @pl.when(last & turns & (z < nz - 1))
            def _():
                for u in mine_of:
                    detour(u, q - 1, u % per_piece).start()

            @pl.when(last & turns & (z == nz - 1))
            def _():
                for u in mine_of:
                    route = LATE_ROUTES[u]
                    (shift(u, lvl + 1) if route == STRAIGHT else detour(u, route, slot_of(u))).start()

    take_peaks(2, y_copies, y_peaks)

    @pl.when(z < nz - 1)
    def _():
        pl.semaphore_wait(z_ack, 2 * (nz - 1 - z))


    def z_copy(slot, zz, half, sender):
        return pltpu.make_async_remote_copy(
            src_ref=peaks.at[3],
            dst_ref=z_peaks.at[slot],
            send_sem=z_send.at[sender],
            recv_sem=z_recv.at[slot],
            device_id=(at(y, lax.rem(zz + nz, nz), x), half * 2 + core),
            device_id_type=MESH,
        )

    ahead = [z_copy(slot, z + slot + 1, half, 2 * slot + half) for slot in range(2) for half in range(2)]
    behind = [z_copy(2, z - 1, half, half) for half in range(2)]

    @pl.when(side == 1)
    def _():
        for copy in ahead:
            copy.start()

    @pl.when(side == 0)
    def _():
        for copy in behind:
            copy.start()

    def rest():
        for i in range(EARLY, CHUNKS):
            links[2][i].start()

    @pl.when(holds & last)
    def _():
        for u in reversed(range(per_piece)):
            shift(u, lvl + 1).start()
        rest()

    def hand_over(act):
        @pl.when((z < nz - 1) & jnp.logical_not(last))
        def _():
            for slot in reversed(range(per_piece)):
                act(slot, forward(slot, per_piece * (x + 1) + slot))

        for route in sorted(set(LATE_ROUTES) - {STRAIGHT}):

            @pl.when((z == nz - 1) & (x == route) & turns)
            def _():
                for u in reversed(range(units)):
                    if LATE_ROUTES[u] == route:
                        act(slot_of(u), forward(slot_of(u), u))

    def take_and_start(slot, copy):
        detour(0, 0, slot).wait_recv()
        copy.start()

    hand_over(take_and_start)

    @pl.when(holds & jnp.logical_not(last))
    def _():
        rest()

    for i in range(CHUNKS):
        hand_on(1, i)
    gathered(1)

    @pl.when(last & turns & (z < nz - 1))
    def _():
        for u in reversed(range(per_piece)):
            shift(u, lvl + 1).start()

    u_high, u_low = split(full[1])
    upper[...] = product(u_high, u_low, solved[...])

    for i in range(CHUNKS):
        hand_on(2, i)
    gathered(2)
    w_high, w_low = split(full[2])
    high[1] = w_high
    low[1] = w_low
    local[4].wait()

    @pl.when(lvl == 0)
    def _():
        below[...] = jnp.zeros_like(below)

    def lower_half(half):
        part = slice(half * rows // 2, (half + 1) * rows // 2)

        @pl.when(lvl > 0)
        def _():
            for u in range(half * units // 2, (half + 1) * units // 2):
                shift(u, lvl).wait_recv()

        return product(high[1, :, part], low[1, :, part], below[part, :])

    lower = lower_half(1)
    best = peaks[3]
    for slot in range(3):
        z_copy(slot, z, side, 0).wait_recv()
        best = jnp.maximum(best, z_peaks[slot])
    factor = 1.0 / jnp.max(best, keepdims=True)
    out_level[0] = (mine_even[...] + upper[:, share:]) * factor
    out_up[0] = upper[:, :share] * factor
    lower = lower + lower_half(0)
    out_level[0] = out_level[0] + lower[:, :share] * factor
    out_down[0] = lower[:, share:] * factor

    for copy in col_copies + x_copies + y_copies + owns:
        copy.wait_send()
    for m in range(3):
        for i in range(CHUNKS):
            links[m][i].wait_send()
            relays[m][i].wait_send()

    @pl.when(side == 1)
    def _():
        for copy in ahead:
            copy.wait_send()

    @pl.when(side == 0)
    def _():
        for copy in behind:
            copy.wait_send()

    @pl.when(jnp.logical_not(last) | turns)
    def _():
        for u in range(units):
            shift(u, lvl).wait_send()

    hand_over(lambda slot, copy: copy.wait_send())


def place_results(level, up, down, out_level, out_up, out_down, sem):
    copies = [
        pltpu.make_async_copy(source, target, sem.at[i])
        for i, (source, target) in enumerate(((level, out_level), (up, out_up), (down, out_down)))
    ]
    for copy in copies:
        copy.start()
    for copy in copies:
        copy.wait()


def per_device(sides, up, level, down):
    rows, share = up.shape[1], up.shape[2]
    ny, nz, nx = sides
    dma = pltpu.SemaphoreType.DMA
    regular = pltpu.SemaphoreType.REGULAR
    tile = (8, share)
    block = jax.ShapeDtypeStruct((1, rows, share), F32)
    results = pl.pallas_call(
        functools.partial(kernel, sides),
        out_shape=(block, block, block),
        in_specs=[pl.BlockSpec(memory_space=pl.ANY)] * 3,
        out_specs=(pl.BlockSpec(memory_space=pltpu.VMEM),) * 3,
        scratch_shapes=[
            pltpu.VMEM((3, rows, rows), F32),
            pltpu.VMEM((2, rows, rows), BF16),
            pltpu.VMEM((2, rows, rows), BF16),
            pltpu.VMEM((rows, 2 * share), F32),
            pltpu.VMEM((rows, share), F32),
            pltpu.VMEM((2, share, share), F32),
            pltpu.VMEM((rows, 2 * share), F32),
            pltpu.VMEM((rows, 2 * share), F32),
            pltpu.VMEM((rows // UNIT // 2, UNIT, 2 * share), F32),
            pltpu.VMEM((rows, 2 * share), F32),
            pltpu.VMEM((4,) + tile, F32),
            pltpu.VMEM((3,) + tile, F32),
            pltpu.VMEM((nx - 1,) + tile, F32),
            pltpu.VMEM((ny - 1,) + tile, F32),
            pltpu.VMEM((3,) + tile, F32),
            dma((8,)),
            dma((3, CHUNKS)),
            dma((3, CHUNKS)),
            dma((3, CHUNKS)),
            dma((3, CHUNKS)),
            dma((3,)),
            dma((3,)),
            dma((rows // UNIT,)),
            dma((rows // UNIT,)),
            dma((rows // UNIT // 2,)),
            dma((rows // UNIT // 2,)),
            dma((3,)),
            dma((3,)),
            dma((nx - 1,)),
            dma((nx - 1,)),
            dma((ny - 1,)),
            dma((ny - 1,)),
            dma((4,)),
            dma((3,)),
            regular,
            regular,
            regular,
            regular,
        ],
        compiler_params=pltpu.CompilerParams(
            collective_id=0, has_side_effects=True, vmem_limit_bytes=40 * 1024 * 1024
        ),
    )(*(pltpu.with_memory_space_constraint(v, pltpu.HBM) for v in (up, level, down)))
    return pl.pallas_call(
        place_results,
        out_shape=(block, block, block),
        in_specs=[pl.BlockSpec(memory_space=pltpu.VMEM)] * 3,
        out_specs=(pl.BlockSpec(memory_space=pl.ANY),) * 3,
        scratch_shapes=[dma((3,))],
        compiler_params=pltpu.CompilerParams(vmem_limit_bytes=8 * 1024 * 1024),
    )(*results)


def solution(mesh, sides=(8, 4, 4)):
    placed = P("lvl", None, "col")
    return jax.shard_map(
        functools.partial(per_device, sides),
        mesh=mesh,
        in_specs=(placed, placed, placed),
        out_specs=(placed, placed, placed),
        check_vma=False,
    )
```

```python
import functools

import jax
import jax.numpy as jnp
from jax import lax
from jax.experimental import pallas as pl
from jax.experimental.pallas import tpu as pltpu
from jax.sharding import PartitionSpec as P

SWEEPS = 2
MESH = pl.DeviceIdType.MESH
F32 = jnp.float32
BF16 = jnp.bfloat16
CHUNKS = 4
EARLY = 1
UNIT = 64
STRAIGHT = -1
LATE_ROUTES = (-1, -1, -1, 1, 0, 0, 2, 2)


def slot_of(u):
    return sum(LATE_ROUTES[v] == LATE_ROUTES[u] for v in range(u))


def split(x):
    high = x.astype(BF16)
    low = (x - high.astype(F32)).astype(BF16)
    return high, low


def dot(a, b):
    return jnp.dot(a, b, preferred_element_type=F32)


def product(a_high, a_low, x):
    x_high, x_low = split(x)
    return dot(a_high, x_high) + (dot(a_high, x_low) + dot(a_low, x_high))


def start_rank(y, ny, first_last):
    rank = jnp.where(2 * y < ny, y, ny + ny // 2 - 1 - y)
    return jnp.where(first_last, jnp.where(y == 0, ny - 1, rank - 1), rank)


def x_rank(x, nx, first_last):
    return jnp.where(first_last, jnp.where(x == 0, nx - 1, x - 1), x)


def kernel(
    sides,
    up,
    level,
    down,
    out_level,
    out_up,
    out_down,
    full,
    high,
    low,
    right,
    mine_even,
    squares,
    solved,
    below,
    hop,
    upper,
    peaks,
    col_peaks,
    x_peaks,
    y_peaks,
    z_peaks,
    local_sem,
    link_send,
    link_recv,
    relay_send,
    relay_recv,
    own_send,
    own_recv,
    shift_send,
    shift_recv,
    hop_recv,
    forward_send,
    col_send,
    col_recv,
    x_send,
    x_recv,
    y_send,
    y_recv,
    z_send,
    z_recv,
    x_ack,
    y_ack,
    z_ack,
    next_ack,
):
    ny, nz, nx = sides
    lvl = lax.axis_index("lvl")
    col = lax.axis_index("col")
    rows, share = up.shape[1], up.shape[2]
    x = lax.rem(lvl, nx)
    run = lvl // nx
    runs = ny * nz
    z = lax.rem(run, nz)
    y = run // nz
    core = lax.rem(col, 2)
    side = col // 2
    partner = col + 1 - 2 * core
    across = lax.rem(col + 2, 4)

    def at(yy, zz, xx):
        return (yy * nz + zz) * nx + xx

    def signal(semaphore, device):
        pl.semaphore_signal(semaphore, inc=1, device_id=device, device_id_type=MESH)

    y_late = (x == 0) & (z == 0) & (col == 0)
    x_late = (y == 0) & (z == 0) & (col == 0)
    rank = start_rank(y, ny, y_late)
    place = x_rank(x, nx, x_late)
    x_group = [lax.rem(x + j, nx) for j in range(1, nx)]
    y_group = [lax.rem(y + j, ny) for j in range(1, ny)]
    z_group = [lax.rem(z + j, nz) for j in range(1, nz)]
    x_devices = [(at(y, z, xx), col) for xx in x_group]
    y_devices = [(at(yy, z, x), col) for yy in y_group]
    col_group = [(lvl, lax.rem(col + j, 4)) for j in range(1, 4)]
    head = (run + 1) * nx
    turns = run < runs - 1
    last = x == nx - 1
    holds = (z == nz - 1) & turns & ((x != 1) | (1 in LATE_ROUTES))

    def columns(c):
        return pl.ds(pl.multiple_of(c * share, share), share)

    mine = columns(col)
    theirs = columns(across)
    blocks = (level.at[1], up.at[0], down.at[0])

    local = [
        pltpu.make_async_copy(level.at[0, mine, :], squares.at[0], local_sem.at[0]),
        pltpu.make_async_copy(level.at[1, mine, :], squares.at[1], local_sem.at[1]),
        pltpu.make_async_copy(up.at[1], right.at[:, 0:share], local_sem.at[2]),
        pltpu.make_async_copy(down.at[1], right.at[:, share : 2 * share], local_sem.at[3]),
        pltpu.make_async_copy(level.at[0], mine_even, local_sem.at[4]),
    ] + [
        pltpu.make_async_copy(blocks[m], full.at[m, :, mine], local_sem.at[5 + m]) for m in range(3)
    ]

    barrier = pltpu.get_barrier_semaphore()
    for device in col_group:
        signal(barrier, device)
    for copy in local:
        copy.start()
    for xx, device in zip(x_group, x_devices):

        @pl.when(x_rank(xx, nx, x_late) > place)
        def _():
            signal(barrier, device)

    for yy, device in zip(y_group, y_devices):

        @pl.when(start_rank(yy, ny, y_late) > rank)
        def _():
            signal(barrier, device)

    for zz in z_group:

        @pl.when(zz > z)
        def _():
            for half in range(2):
                signal(barrier, (at(y, zz, x), half * 2 + core))

    @pl.when((x == 0) & (z == 0) & (run > 0))
    def _():
        for xx in range(nx):
            signal(barrier, (lvl - nx + xx, col))

    local[0].wait()
    local[1].wait()
    row = lax.broadcasted_iota(jnp.int32, (share, share), 0)
    column = lax.broadcasted_iota(jnp.int32, (share, share), 1)
    diagonal = row == column
    rates = jnp.where(diagonal, jnp.maximum(-squares[0], -squares[1]), -jnp.inf)
    peaks[0] = jnp.max(rates.reshape(share // 8, 8, share), axis=0)

    expected = 3 + place + rank + 2 * z
    expected = expected + jnp.where(turns & (z == nz - 1), 1, 0)
    pl.semaphore_wait(barrier, expected)

    def send_peaks(stage, group, slots, send, recv):
        copies = []
        for j, device in enumerate(group):
            copies.append(
                pltpu.make_async_remote_copy(
                    src_ref=peaks.at[stage],
                    dst_ref=slots.at[j],
                    send_sem=send.at[j],
                    recv_sem=recv.at[j],
                    device_id=device,
                    device_id_type=MESH,
                )
            )
            copies[-1].start()
        return copies

    def take_peaks(stage, copies, slots):
        best = peaks[stage]
        for j, copy in enumerate(copies):
            copy.wait_recv()
            best = jnp.maximum(best, slots[j])
        peaks[stage + 1] = best

    step = rows // CHUNKS

    def link(m, i):
        part = pl.ds(i * step, step)
        return pltpu.make_async_remote_copy(
            src_ref=blocks[m].at[part, :],
            dst_ref=full.at[m, part, mine],
            send_sem=link_send.at[m, i],
            recv_sem=link_recv.at[m, i],
            device_id=(lvl, across),
            device_id_type=MESH,
        )

    def relay(m, i):
        part = pl.ds(i * step, step)
        return pltpu.make_async_remote_copy(
            src_ref=full.at[m, part, theirs],
            dst_ref=full.at[m, part, theirs],
            send_sem=relay_send.at[m, i],
            recv_sem=relay_recv.at[m, i],
            device_id=(lvl, partner),
            device_id_type=MESH,
        )

    def own(m):
        return pltpu.make_async_remote_copy(
            src_ref=blocks[m],
            dst_ref=full.at[m, :, mine],
            send_sem=own_send.at[m],
            recv_sem=own_recv.at[m],
            device_id=(lvl, partner),
            device_id_type=MESH,
        )

    links = [[link(m, i) for i in range(CHUNKS)] for m in range(3)]
    relays = [[relay(m, i) for i in range(CHUNKS)] for m in range(3)]
    owns = [own(m) for m in range(3)]

    col_copies = send_peaks(0, col_group, col_peaks, col_send, col_recv)
    for i in range(CHUNKS):
        links[0][i].start()
    for m in range(3):
        owns[m].start()

    for xx, device in zip(x_group, x_devices):

        @pl.when(x_rank(xx, nx, x_late) < place)
        def _():
            signal(x_ack, device)

    for yy, device in zip(y_group, y_devices):

        @pl.when(start_rank(yy, ny, y_late) < rank)
        def _():
            signal(y_ack, device)

    for zz in z_group:

        @pl.when(zz < z)
        def _():
            for half in range(2):
                signal(z_ack, (at(y, zz, x), half * 2 + core))

    @pl.when((x == 0) & (z > 0))
    def _():
        signal(next_ack, (lvl - nx, col))

    def hand_on(m, i):
        links[m][i].wait_recv()
        relays[m][i].start()

    def gathered(m):
        local[5 + m].wait()
        owns[m].wait_recv()
        for i in range(CHUNKS):
            relays[m][i].wait_recv()

    take_peaks(0, col_copies, col_peaks)

    @pl.when(place < nx - 1)
    def _():
        pl.semaphore_wait(x_ack, nx - 1 - place)

    x_copies = send_peaks(1, x_devices, x_peaks, x_send, x_recv)
    for i in range(CHUNKS - 2):
        hand_on(0, i)

    @pl.when((x == 0) & (z < nz - 1))
    def _():
        pl.semaphore_wait(next_ack, 1)
        for xx in range(1, nx):
            signal(next_ack, (lvl + xx, col))

    hand_on(0, CHUNKS - 2)
    for i in range(CHUNKS):
        links[1][i].start()
    hand_on(0, CHUNKS - 1)
    take_peaks(1, x_copies, x_peaks)

    @pl.when(rank < ny - 1)
    def _():
        pl.semaphore_wait(y_ack, ny - 1 - rank)

    y_copies = send_peaks(2, y_devices, y_peaks, y_send, y_recv)
    gathered(0)
    local[2].wait()
    local[3].wait()
    for i in range(EARLY):
        links[2][i].start()

    @pl.when(jnp.logical_not(holds))
    def _():
        for i in range(EARLY, CHUNKS):
            links[2][i].start()

    inverse = []
    for s in range(rows // share):
        part = slice(s * share, (s + 1) * share)
        square = full[0, part, part]
        inverse.append(1.0 / jnp.sum(jnp.where(diagonal, -square, 0.0), axis=1, keepdims=True))
        high[0, part, :], low[0, part, :] = split(full[0, part, :])
        high[0, part, part], low[0, part, part] = split(jnp.where(diagonal, 0.0, square))
    every = jnp.concatenate(inverse, axis=0)
    sides_of = right[...]
    guess = sides_of * every
    for _ in range(SWEEPS - 1):
        guess = (sides_of + product(high[0], low[0], guess)) * every
    guess_high, guess_low = split(guess)

    units = rows // UNIT
    per_piece = units // (rows // share)

    def unit(u):
        return slice(u * UNIT, (u + 1) * UNIT)

    def shift(u, device):
        return pltpu.make_async_remote_copy(
            src_ref=solved.at[unit(u), :],
            dst_ref=below.at[unit(u), :],
            send_sem=shift_send.at[u],
            recv_sem=shift_recv.at[u],
            device_id=(device, col),
            device_id_type=MESH,
        )

    def detour(u, target, slot):
        return pltpu.make_async_remote_copy(
            src_ref=solved.at[unit(u), :],
            dst_ref=hop.at[slot],
            send_sem=shift_send.at[u],
            recv_sem=hop_recv.at[slot],
            device_id=(at(y, z, target), col),
            device_id_type=MESH,
        )

    def forward(slot, u):
        return pltpu.make_async_remote_copy(
            src_ref=hop.at[slot],
            dst_ref=below.at[pl.ds(pl.multiple_of(u * UNIT, UNIT), UNIT), :],
            send_sem=forward_send.at[slot],
            recv_sem=shift_recv.at[u],
            device_id=(head, col),
            device_id_type=MESH,
        )

    @pl.when((x > 0) & (z < nz - 1))
    def _():
        pl.semaphore_wait(next_ack, 1)

    pieces = rows // share
    for q in reversed(range(pieces)):
        part = slice(q * share, (q + 1) * share)
        term = dot(high[0, part, :], guess_high) + (
            dot(high[0, part, :], guess_low) + dot(low[0, part, :], guess_high)
        )
        solved[part, :] = (right[part, :] + term) * inverse[q]

        mine_of = [u for u in reversed(range(units)) if u * UNIT // share == q]

        @pl.when(jnp.logical_not(last))
        def _():
            for u in mine_of:
                shift(u, lvl + 1).start()

        if q > 0:

            @pl.when(last & turns & (z < nz - 1))
            def _():
                for u in mine_of:
                    detour(u, q - 1, u % per_piece).start()

        @pl.when(last & turns & (z == nz - 1))
        def _():
            for u in mine_of:
                route = LATE_ROUTES[u]
                (shift(u, lvl + 1) if route == STRAIGHT else detour(u, route, slot_of(u))).start()

    take_peaks(2, y_copies, y_peaks)

    @pl.when(z < nz - 1)
    def _():
        pl.semaphore_wait(z_ack, 2 * (nz - 1 - z))


    def z_copy(slot, zz, half, sender):
        return pltpu.make_async_remote_copy(
            src_ref=peaks.at[3],
            dst_ref=z_peaks.at[slot],
            send_sem=z_send.at[sender],
            recv_sem=z_recv.at[slot],
            device_id=(at(y, lax.rem(zz + nz, nz), x), half * 2 + core),
            device_id_type=MESH,
        )

    ahead = [z_copy(slot, z + slot + 1, half, 2 * slot + half) for slot in range(2) for half in range(2)]
    behind = [z_copy(2, z - 1, half, half) for half in range(2)]

    @pl.when(side == 1)
    def _():
        for copy in ahead:
            copy.start()

    @pl.when(side == 0)
    def _():
        for copy in behind:
            copy.start()

    def rest():
        for i in range(EARLY, CHUNKS):
            links[2][i].start()

    @pl.when(holds & last)
    def _():
        rest()

    def hand_over(act):
        @pl.when((z < nz - 1) & jnp.logical_not(last))
        def _():
            for slot in reversed(range(per_piece)):
                act(slot, forward(slot, per_piece * (x + 1) + slot))

        for route in sorted(set(LATE_ROUTES) - {STRAIGHT}):

            @pl.when((z == nz - 1) & (x == route) & turns)
            def _():
                for u in reversed(range(units)):
                    if LATE_ROUTES[u] == route:
                        act(slot_of(u), forward(slot_of(u), u))

    def take_and_start(slot, copy):
        detour(0, 0, slot).wait_recv()
        copy.start()

    hand_over(take_and_start)

    @pl.when(holds & jnp.logical_not(last))
    def _():
        rest()

    for i in range(CHUNKS):
        hand_on(1, i)
    gathered(1)

    @pl.when(last & turns & (z < nz - 1))
    def _():
        for u in reversed(range(per_piece)):
            shift(u, lvl + 1).start()

    u_high, u_low = split(full[1])
    upper[...] = product(u_high, u_low, solved[...])

    for i in range(CHUNKS):
        hand_on(2, i)
    gathered(2)
    w_high, w_low = split(full[2])
    high[1] = w_high
    low[1] = w_low
    local[4].wait()

    @pl.when(lvl == 0)
    def _():
        below[...] = jnp.zeros_like(below)

    def lower_half(half):
        part = slice(half * rows // 2, (half + 1) * rows // 2)

        @pl.when(lvl > 0)
        def _():
            for u in range(half * units // 2, (half + 1) * units // 2):
                shift(u, lvl).wait_recv()

        return product(high[1, :, part], low[1, :, part], below[part, :])

    lower = lower_half(1)
    best = peaks[3]
    for slot in range(3):
        z_copy(slot, z, side, 0).wait_recv()
        best = jnp.maximum(best, z_peaks[slot])
    factor = 1.0 / jnp.max(best, keepdims=True)
    out_level[0] = (mine_even[...] + upper[:, share:]) * factor
    out_up[0] = upper[:, :share] * factor
    lower = lower + lower_half(0)
    out_level[0] = out_level[0] + lower[:, :share] * factor
    out_down[0] = lower[:, share:] * factor

    for copy in col_copies + x_copies + y_copies + owns:
        copy.wait_send()
    for m in range(3):
        for i in range(CHUNKS):
            links[m][i].wait_send()
            relays[m][i].wait_send()

    @pl.when(side == 1)
    def _():
        for copy in ahead:
            copy.wait_send()

    @pl.when(side == 0)
    def _():
        for copy in behind:
            copy.wait_send()

    @pl.when(jnp.logical_not(last) | turns)
    def _():
        for u in range(units):
            shift(u, lvl).wait_send()

    hand_over(lambda slot, copy: copy.wait_send())


def place_results(level, up, down, out_level, out_up, out_down, sem):
    copies = [
        pltpu.make_async_copy(source, target, sem.at[i])
        for i, (source, target) in enumerate(((level, out_level), (up, out_up), (down, out_down)))
    ]
    for copy in copies:
        copy.start()
    for copy in copies:
        copy.wait()


def per_device(sides, up, level, down):
    rows, share = up.shape[1], up.shape[2]
    ny, nz, nx = sides
    dma = pltpu.SemaphoreType.DMA
    regular = pltpu.SemaphoreType.REGULAR
    tile = (8, share)
    block = jax.ShapeDtypeStruct((1, rows, share), F32)
    results = pl.pallas_call(
        functools.partial(kernel, sides),
        out_shape=(block, block, block),
        in_specs=[pl.BlockSpec(memory_space=pl.ANY)] * 3,
        out_specs=(pl.BlockSpec(memory_space=pltpu.VMEM),) * 3,
        scratch_shapes=[
            pltpu.VMEM((3, rows, rows), F32),
            pltpu.VMEM((2, rows, rows), BF16),
            pltpu.VMEM((2, rows, rows), BF16),
            pltpu.VMEM((rows, 2 * share), F32),
            pltpu.VMEM((rows, share), F32),
            pltpu.VMEM((2, share, share), F32),
            pltpu.VMEM((rows, 2 * share), F32),
            pltpu.VMEM((rows, 2 * share), F32),
            pltpu.VMEM((rows // UNIT // 2, UNIT, 2 * share), F32),
            pltpu.VMEM((rows, 2 * share), F32),
            pltpu.VMEM((4,) + tile, F32),
            pltpu.VMEM((3,) + tile, F32),
            pltpu.VMEM((nx - 1,) + tile, F32),
            pltpu.VMEM((ny - 1,) + tile, F32),
            pltpu.VMEM((3,) + tile, F32),
            dma((8,)),
            dma((3, CHUNKS)),
            dma((3, CHUNKS)),
            dma((3, CHUNKS)),
            dma((3, CHUNKS)),
            dma((3,)),
            dma((3,)),
            dma((rows // UNIT,)),
            dma((rows // UNIT,)),
            dma((rows // UNIT // 2,)),
            dma((rows // UNIT // 2,)),
            dma((3,)),
            dma((3,)),
            dma((nx - 1,)),
            dma((nx - 1,)),
            dma((ny - 1,)),
            dma((ny - 1,)),
            dma((4,)),
            dma((3,)),
            regular,
            regular,
            regular,
            regular,
        ],
        compiler_params=pltpu.CompilerParams(
            collective_id=0, has_side_effects=True, vmem_limit_bytes=40 * 1024 * 1024
        ),
    )(*(pltpu.with_memory_space_constraint(v, pltpu.HBM) for v in (up, level, down)))
    return pl.pallas_call(
        place_results,
        out_shape=(block, block, block),
        in_specs=[pl.BlockSpec(memory_space=pltpu.VMEM)] * 3,
        out_specs=(pl.BlockSpec(memory_space=pl.ANY),) * 3,
        scratch_shapes=[dma((3,))],
        compiler_params=pltpu.CompilerParams(vmem_limit_bytes=8 * 1024 * 1024),
    )(*results)


def solution(mesh, sides=(8, 4, 4)):
    placed = P("lvl", None, "col")
    return jax.shard_map(
        functools.partial(per_device, sides),
        mesh=mesh,
        in_specs=(placed, placed, placed),
        out_specs=(placed, placed, placed),
        check_vma=False,
    )
```

```python
import functools

import jax
import jax.numpy as jnp
from jax import lax
from jax.experimental import pallas as pl
from jax.experimental.pallas import tpu as pltpu
from jax.sharding import PartitionSpec as P

SWEEPS = 2
MESH = pl.DeviceIdType.MESH
F32 = jnp.float32
BF16 = jnp.bfloat16
CHUNKS = 8
EARLY = 2
UNIT = 64
STRAIGHT = -1
LATE_ROUTES = (-1, -1, -1, 1, 0, 0, 2, 2)


def slot_of(u):
    return sum(LATE_ROUTES[v] == LATE_ROUTES[u] for v in range(u))


def split(x):
    high = x.astype(BF16)
    low = (x - high.astype(F32)).astype(BF16)
    return high, low


def dot(a, b):
    return jnp.dot(a, b, preferred_element_type=F32)


def product(a_high, a_low, x):
    x_high, x_low = split(x)
    return dot(a_high, x_high) + (dot(a_high, x_low) + dot(a_low, x_high))


def start_rank(y, ny, first_last):
    rank = jnp.where(2 * y < ny, y, ny + ny // 2 - 1 - y)
    return jnp.where(first_last, jnp.where(y == 0, ny - 1, rank - 1), rank)


def x_rank(x, nx, first_last):
    return jnp.where(first_last, jnp.where(x == 0, nx - 1, x - 1), x)


def kernel(
    sides,
    up,
    level,
    down,
    out_level,
    out_up,
    out_down,
    full,
    high,
    low,
    right,
    mine_even,
    squares,
    solved,
    below,
    hop,
    upper,
    peaks,
    col_peaks,
    x_peaks,
    y_peaks,
    z_peaks,
    local_sem,
    link_send,
    link_recv,
    relay_send,
    relay_recv,
    own_send,
    own_recv,
    shift_send,
    shift_recv,
    hop_recv,
    forward_send,
    col_send,
    col_recv,
    x_send,
    x_recv,
    y_send,
    y_recv,
    z_send,
    z_recv,
    x_ack,
    y_ack,
    z_ack,
    next_ack,
):
    ny, nz, nx = sides
    lvl = lax.axis_index("lvl")
    col = lax.axis_index("col")
    rows, share = up.shape[1], up.shape[2]
    x = lax.rem(lvl, nx)
    run = lvl // nx
    runs = ny * nz
    z = lax.rem(run, nz)
    y = run // nz
    core = lax.rem(col, 2)
    side = col // 2
    partner = col + 1 - 2 * core
    across = lax.rem(col + 2, 4)

    def at(yy, zz, xx):
        return (yy * nz + zz) * nx + xx

    def signal(semaphore, device):
        pl.semaphore_signal(semaphore, inc=1, device_id=device, device_id_type=MESH)

    y_late = (x == 0) & (z == 0) & (col == 0)
    x_late = (y == 0) & (z == 0) & (col == 0)
    rank = start_rank(y, ny, y_late)
    place = x_rank(x, nx, x_late)
    x_group = [lax.rem(x + j, nx) for j in range(1, nx)]
    y_group = [lax.rem(y + j, ny) for j in range(1, ny)]
    z_group = [lax.rem(z + j, nz) for j in range(1, nz)]
    x_devices = [(at(y, z, xx), col) for xx in x_group]
    y_devices = [(at(yy, z, x), col) for yy in y_group]
    col_group = [(lvl, lax.rem(col + j, 4)) for j in range(1, 4)]
    head = (run + 1) * nx
    turns = run < runs - 1
    last = x == nx - 1
    holds = (z == nz - 1) & turns & ((x != 1) | (1 in LATE_ROUTES))

    def columns(c):
        return pl.ds(pl.multiple_of(c * share, share), share)

    mine = columns(col)
    theirs = columns(across)
    blocks = (level.at[1], up.at[0], down.at[0])

    local = [
        pltpu.make_async_copy(level.at[0, mine, :], squares.at[0], local_sem.at[0]),
        pltpu.make_async_copy(level.at[1, mine, :], squares.at[1], local_sem.at[1]),
        pltpu.make_async_copy(up.at[1], right.at[:, 0:share], local_sem.at[2]),
        pltpu.make_async_copy(down.at[1], right.at[:, share : 2 * share], local_sem.at[3]),
        pltpu.make_async_copy(level.at[0], mine_even, local_sem.at[4]),
    ] + [
        pltpu.make_async_copy(blocks[m], full.at[m, :, mine], local_sem.at[5 + m]) for m in range(3)
    ]

    barrier = pltpu.get_barrier_semaphore()
    for device in col_group:
        signal(barrier, device)
    for copy in local:
        copy.start()
    for xx, device in zip(x_group, x_devices):

        @pl.when(x_rank(xx, nx, x_late) > place)
        def _():
            signal(barrier, device)

    for yy, device in zip(y_group, y_devices):

        @pl.when(start_rank(yy, ny, y_late) > rank)
        def _():
            signal(barrier, device)

    for zz in z_group:

        @pl.when(zz > z)
        def _():
            for half in range(2):
                signal(barrier, (at(y, zz, x), half * 2 + core))

    @pl.when((x == 0) & (z == 0) & (run > 0))
    def _():
        for xx in range(nx):
            signal(barrier, (lvl - nx + xx, col))

    local[0].wait()
    local[1].wait()
    row = lax.broadcasted_iota(jnp.int32, (share, share), 0)
    column = lax.broadcasted_iota(jnp.int32, (share, share), 1)
    diagonal = row == column
    rates = jnp.where(diagonal, jnp.maximum(-squares[0], -squares[1]), -jnp.inf)
    peaks[0] = jnp.max(rates.reshape(share // 8, 8, share), axis=0)

    expected = 3 + place + rank + 2 * z
    expected = expected + jnp.where(turns & (z == nz - 1), 1, 0)
    pl.semaphore_wait(barrier, expected)

    def send_peaks(stage, group, slots, send, recv):
        copies = []
        for j, device in enumerate(group):
            copies.append(
                pltpu.make_async_remote_copy(
                    src_ref=peaks.at[stage],
                    dst_ref=slots.at[j],
                    send_sem=send.at[j],
                    recv_sem=recv.at[j],
                    device_id=device,
                    device_id_type=MESH,
                )
            )
            copies[-1].start()
        return copies

    def take_peaks(stage, copies, slots):
        best = peaks[stage]
        for j, copy in enumerate(copies):
            copy.wait_recv()
            best = jnp.maximum(best, slots[j])
        peaks[stage + 1] = best

    step = rows // CHUNKS

    def link(m, i):
        part = pl.ds(i * step, step)
        return pltpu.make_async_remote_copy(
            src_ref=blocks[m].at[part, :],
            dst_ref=full.at[m, part, mine],
            send_sem=link_send.at[m, i],
            recv_sem=link_recv.at[m, i],
            device_id=(lvl, across),
            device_id_type=MESH,
        )

    def relay(m, i):
        part = pl.ds(i * step, step)
        return pltpu.make_async_remote_copy(
            src_ref=full.at[m, part, theirs],
            dst_ref=full.at[m, part, theirs],
            send_sem=relay_send.at[m, i],
            recv_sem=relay_recv.at[m, i],
            device_id=(lvl, partner),
            device_id_type=MESH,
        )

    def own(m):
        return pltpu.make_async_remote_copy(
            src_ref=blocks[m],
            dst_ref=full.at[m, :, mine],
            send_sem=own_send.at[m],
            recv_sem=own_recv.at[m],
            device_id=(lvl, partner),
            device_id_type=MESH,
        )

    links = [[link(m, i) for i in range(CHUNKS)] for m in range(3)]
    relays = [[relay(m, i) for i in range(CHUNKS)] for m in range(3)]
    owns = [own(m) for m in range(3)]

    col_copies = send_peaks(0, col_group, col_peaks, col_send, col_recv)
    for i in range(CHUNKS):
        links[0][i].start()
    for m in range(3):
        owns[m].start()

    for xx, device in zip(x_group, x_devices):

        @pl.when(x_rank(xx, nx, x_late) < place)
        def _():
            signal(x_ack, device)

    for yy, device in zip(y_group, y_devices):

        @pl.when(start_rank(yy, ny, y_late) < rank)
        def _():
            signal(y_ack, device)

    for zz in z_group:

        @pl.when(zz < z)
        def _():
            for half in range(2):
                signal(z_ack, (at(y, zz, x), half * 2 + core))

    @pl.when((x == 0) & (z > 0))
    def _():
        signal(next_ack, (lvl - nx, col))

    def hand_on(m, i):
        links[m][i].wait_recv()
        relays[m][i].start()

    def gathered(m):
        local[5 + m].wait()
        owns[m].wait_recv()
        for i in range(CHUNKS):
            relays[m][i].wait_recv()

    take_peaks(0, col_copies, col_peaks)

    @pl.when(place < nx - 1)
    def _():
        pl.semaphore_wait(x_ack, nx - 1 - place)

    x_copies = send_peaks(1, x_devices, x_peaks, x_send, x_recv)
    for i in range(CHUNKS - 2):
        hand_on(0, i)

    @pl.when((x == 0) & (z < nz - 1))
    def _():
        pl.semaphore_wait(next_ack, 1)
        for xx in range(1, nx):
            signal(next_ack, (lvl + xx, col))

    hand_on(0, CHUNKS - 2)
    for i in range(CHUNKS):
        links[1][i].start()
    hand_on(0, CHUNKS - 1)
    take_peaks(1, x_copies, x_peaks)

    @pl.when(rank < ny - 1)
    def _():
        pl.semaphore_wait(y_ack, ny - 1 - rank)

    y_copies = send_peaks(2, y_devices, y_peaks, y_send, y_recv)
    gathered(0)
    local[2].wait()
    local[3].wait()
    for i in range(EARLY):
        links[2][i].start()

    @pl.when(jnp.logical_not(holds))
    def _():
        for i in range(EARLY, CHUNKS):
            links[2][i].start()

    inverse = []
    for s in range(rows // share):
        part = slice(s * share, (s + 1) * share)
        square = full[0, part, part]
        inverse.append(1.0 / jnp.sum(jnp.where(diagonal, -square, 0.0), axis=1, keepdims=True))
        high[0, part, :], low[0, part, :] = split(full[0, part, :])
        high[0, part, part], low[0, part, part] = split(jnp.where(diagonal, 0.0, square))
    every = jnp.concatenate(inverse, axis=0)
    sides_of = right[...]
    guess = sides_of * every
    for _ in range(SWEEPS - 1):
        guess = (sides_of + product(high[0], low[0], guess)) * every
    guess_high, guess_low = split(guess)

    units = rows // UNIT
    per_piece = units // (rows // share)

    def unit(u):
        return slice(u * UNIT, (u + 1) * UNIT)

    def shift(u, device):
        return pltpu.make_async_remote_copy(
            src_ref=solved.at[unit(u), :],
            dst_ref=below.at[unit(u), :],
            send_sem=shift_send.at[u],
            recv_sem=shift_recv.at[u],
            device_id=(device, col),
            device_id_type=MESH,
        )

    def detour(u, target, slot):
        return pltpu.make_async_remote_copy(
            src_ref=solved.at[unit(u), :],
            dst_ref=hop.at[slot],
            send_sem=shift_send.at[u],
            recv_sem=hop_recv.at[slot],
            device_id=(at(y, z, target), col),
            device_id_type=MESH,
        )

    def forward(slot, u):
        return pltpu.make_async_remote_copy(
            src_ref=hop.at[slot],
            dst_ref=below.at[pl.ds(pl.multiple_of(u * UNIT, UNIT), UNIT), :],
            send_sem=forward_send.at[slot],
            recv_sem=shift_recv.at[u],
            device_id=(head, col),
            device_id_type=MESH,
        )

    @pl.when((x > 0) & (z < nz - 1))
    def _():
        pl.semaphore_wait(next_ack, 1)

    pieces = rows // share
    for q in reversed(range(pieces)):
        part = slice(q * share, (q + 1) * share)
        term = dot(high[0, part, :], guess_high) + (
            dot(high[0, part, :], guess_low) + dot(low[0, part, :], guess_high)
        )
        solved[part, :] = (right[part, :] + term) * inverse[q]

        mine_of = [u for u in reversed(range(units)) if u * UNIT // share == q]

        @pl.when(jnp.logical_not(last))
        def _():
            for u in mine_of:
                shift(u, lvl + 1).start()

        if q > 0:

            @pl.when(last & turns & (z < nz - 1))
            def _():
                for u in mine_of:
                    detour(u, q - 1, u % per_piece).start()

        @pl.when(last & turns & (z == nz - 1))
        def _():
            for u in mine_of:
                route = LATE_ROUTES[u]
                (shift(u, lvl + 1) if route == STRAIGHT else detour(u, route, slot_of(u))).start()

    take_peaks(2, y_copies, y_peaks)

    @pl.when(z < nz - 1)
    def _():
        pl.semaphore_wait(z_ack, 2 * (nz - 1 - z))


    def z_copy(slot, zz, half, sender):
        return pltpu.make_async_remote_copy(
            src_ref=peaks.at[3],
            dst_ref=z_peaks.at[slot],
            send_sem=z_send.at[sender],
            recv_sem=z_recv.at[slot],
            device_id=(at(y, lax.rem(zz + nz, nz), x), half * 2 + core),
            device_id_type=MESH,
        )

    ahead = [z_copy(slot, z + slot + 1, half, 2 * slot + half) for slot in range(2) for half in range(2)]
    behind = [z_copy(2, z - 1, half, half) for half in range(2)]

    @pl.when(side == 1)
    def _():
        for copy in ahead:
            copy.start()

    @pl.when(side == 0)
    def _():
        for copy in behind:
            copy.start()

    def rest():
        for i in range(EARLY, CHUNKS):
            links[2][i].start()

    @pl.when(holds & last)
    def _():
        rest()

    def hand_over(act):
        @pl.when((z < nz - 1) & jnp.logical_not(last))
        def _():
            for slot in reversed(range(per_piece)):
                act(slot, forward(slot, per_piece * (x + 1) + slot))

        for route in sorted(set(LATE_ROUTES) - {STRAIGHT}):

            @pl.when((z == nz - 1) & (x == route) & turns)
            def _():
                for u in reversed(range(units)):
                    if LATE_ROUTES[u] == route:
                        act(slot_of(u), forward(slot_of(u), u))

    def take_and_start(slot, copy):
        detour(0, 0, slot).wait_recv()
        copy.start()

    hand_over(take_and_start)

    @pl.when(holds & jnp.logical_not(last))
    def _():
        rest()

    for i in range(CHUNKS):
        hand_on(1, i)
    gathered(1)

    @pl.when(last & turns & (z < nz - 1))
    def _():
        for u in reversed(range(per_piece)):
            shift(u, lvl + 1).start()

    u_high, u_low = split(full[1])
    upper[...] = product(u_high, u_low, solved[...])

    for i in range(CHUNKS):
        hand_on(2, i)
    gathered(2)
    w_high, w_low = split(full[2])
    high[1] = w_high
    low[1] = w_low
    local[4].wait()

    @pl.when(lvl == 0)
    def _():
        below[...] = jnp.zeros_like(below)

    def lower_half(half):
        part = slice(half * rows // 2, (half + 1) * rows // 2)

        @pl.when(lvl > 0)
        def _():
            for u in range(half * units // 2, (half + 1) * units // 2):
                shift(u, lvl).wait_recv()

        return product(high[1, :, part], low[1, :, part], below[part, :])

    lower = lower_half(1)
    best = peaks[3]
    for slot in range(3):
        z_copy(slot, z, side, 0).wait_recv()
        best = jnp.maximum(best, z_peaks[slot])
    factor = 1.0 / jnp.max(best, keepdims=True)
    out_level[0] = (mine_even[...] + upper[:, share:]) * factor
    out_up[0] = upper[:, :share] * factor
    lower = lower + lower_half(0)
    out_level[0] = out_level[0] + lower[:, :share] * factor
    out_down[0] = lower[:, share:] * factor

    for copy in col_copies + x_copies + y_copies + owns:
        copy.wait_send()
    for m in range(3):
        for i in range(CHUNKS):
            links[m][i].wait_send()
            relays[m][i].wait_send()

    @pl.when(side == 1)
    def _():
        for copy in ahead:
            copy.wait_send()

    @pl.when(side == 0)
    def _():
        for copy in behind:
            copy.wait_send()

    @pl.when(jnp.logical_not(last) | turns)
    def _():
        for u in range(units):
            shift(u, lvl).wait_send()

    hand_over(lambda slot, copy: copy.wait_send())


def place_results(level, up, down, out_level, out_up, out_down, sem):
    copies = [
        pltpu.make_async_copy(source, target, sem.at[i])
        for i, (source, target) in enumerate(((level, out_level), (up, out_up), (down, out_down)))
    ]
    for copy in copies:
        copy.start()
    for copy in copies:
        copy.wait()


def per_device(sides, up, level, down):
    rows, share = up.shape[1], up.shape[2]
    ny, nz, nx = sides
    dma = pltpu.SemaphoreType.DMA
    regular = pltpu.SemaphoreType.REGULAR
    tile = (8, share)
    block = jax.ShapeDtypeStruct((1, rows, share), F32)
    results = pl.pallas_call(
        functools.partial(kernel, sides),
        out_shape=(block, block, block),
        in_specs=[pl.BlockSpec(memory_space=pl.ANY)] * 3,
        out_specs=(pl.BlockSpec(memory_space=pltpu.VMEM),) * 3,
        scratch_shapes=[
            pltpu.VMEM((3, rows, rows), F32),
            pltpu.VMEM((2, rows, rows), BF16),
            pltpu.VMEM((2, rows, rows), BF16),
            pltpu.VMEM((rows, 2 * share), F32),
            pltpu.VMEM((rows, share), F32),
            pltpu.VMEM((2, share, share), F32),
            pltpu.VMEM((rows, 2 * share), F32),
            pltpu.VMEM((rows, 2 * share), F32),
            pltpu.VMEM((rows // UNIT // 2, UNIT, 2 * share), F32),
            pltpu.VMEM((rows, 2 * share), F32),
            pltpu.VMEM((4,) + tile, F32),
            pltpu.VMEM((3,) + tile, F32),
            pltpu.VMEM((nx - 1,) + tile, F32),
            pltpu.VMEM((ny - 1,) + tile, F32),
            pltpu.VMEM((3,) + tile, F32),
            dma((8,)),
            dma((3, CHUNKS)),
            dma((3, CHUNKS)),
            dma((3, CHUNKS)),
            dma((3, CHUNKS)),
            dma((3,)),
            dma((3,)),
            dma((rows // UNIT,)),
            dma((rows // UNIT,)),
            dma((rows // UNIT // 2,)),
            dma((rows // UNIT // 2,)),
            dma((3,)),
            dma((3,)),
            dma((nx - 1,)),
            dma((nx - 1,)),
            dma((ny - 1,)),
            dma((ny - 1,)),
            dma((4,)),
            dma((3,)),
            regular,
            regular,
            regular,
            regular,
        ],
        compiler_params=pltpu.CompilerParams(
            collective_id=0, has_side_effects=True, vmem_limit_bytes=40 * 1024 * 1024
        ),
    )(*(pltpu.with_memory_space_constraint(v, pltpu.HBM) for v in (up, level, down)))
    return pl.pallas_call(
        place_results,
        out_shape=(block, block, block),
        in_specs=[pl.BlockSpec(memory_space=pltpu.VMEM)] * 3,
        out_specs=(pl.BlockSpec(memory_space=pl.ANY),) * 3,
        scratch_shapes=[dma((3,))],
        compiler_params=pltpu.CompilerParams(vmem_limit_bytes=8 * 1024 * 1024),
    )(*results)


def solution(mesh, sides=(8, 4, 4)):
    placed = P("lvl", None, "col")
    return jax.shard_map(
        functools.partial(per_device, sides),
        mesh=mesh,
        in_specs=(placed, placed, placed),
        out_specs=(placed, placed, placed),
        check_vma=False,
    )
```
